32 devices in a mesh: grp: 2 (over y), sec: 4 (over z), blk: 2 (over x), op: 2 (over core).
Axes of the slice: x: 2, y: 2, z: 4, core: 2. Of those that a mesh axis runs over, the one named last changes fastest.
Arguments:
- ground_state: bfloat16 [48, 512, 512], P(('grp', 'sec'), 'blk'), parts along dimension 0, may hold values from -6 to 6
- op_matrices: bfloat16 [16, 512, 512], P(('grp', 'op')), parts along dimension 0, may hold values from -0.25 to 0.25
- shift_map: int32 [16, 24], P('grp'), parts along dimension 0, may hold values from 0 to 23, as said below
- new_slot: int32 [48], P('grp'), parts along dimension 0, may hold values from 0 to 23, as said below
- env_ground: bfloat16 [48, 512, 512], P(('grp', 'sec'), 'blk'), parts along dimension 0, may hold values from -0.25 to 0.25
- env_src: int32 [48, 3], P('grp'), parts along dimension 0, may hold values from 0 to 23, as said below
- env_coef: float32 [48, 3], P('grp'), parts along dimension 0, may hold values from 0.3 to 1
Outputs:
- grown_env: bfloat16 [16, 24, 512, 512], P(('grp', 'op'), 'sec', 'blk'), parts along dimension 0
The draws below stay inside these ranges and needn't reach their ends.
There are 2 independent parts, one for each index of `grp`. The reference program is written for one: setup_inputs(seed, part) draws one part's arguments, and reference() takes and returns one part's arrays. A program takes and returns all parts, laid end to end along the dimension named above; each array names one. Nothing has to cross between parts.
Inputs may be any that keep to these rules, and one draw needn't show every extreme that they name: Each row o maps the 24 ground sectors one to one onto the N+1 sectors. Within each group of 4 consecutive operators, among the pairs (o, s) with one value of s // 6, at most 7 have new_slot[shift_map[o, s]] // 6 equal to one value, and 7 is reached for every value of s // 6. A permutation: N+1 sector t is stored at slot new_slot[t]. For the N+1 sectors t with one value of new_slot[t] // 6, at most 6 of the entries env_src[t, k] have one value of env_src[t, k] // 6, and 6 is reached for every value of new_slot[t] // 6.
All inputs are finite; a program needn't handle non-finite values.
Results may differ from the reference program's by a relative error of at most 0.0057.
Values may be sent and summed in bfloat16 or wider, within the bound.
No kernel may reach another device: no remote copies, remote signals or barrier semaphores. Data moves between devices by JAX's collectives and lax.ppermute only.
A program may use at most 64 MiB of HBM per device.

```python
import jax
import jax.numpy as jnp
from jax import lax

DIM = 512
SEC_DEV = 6
OPS_DEV = 4
ENV_K = 3
SECTORS = 24
OPS = 8
CAP = 7
ECAP = 6


def spread_offsets(key, total_count, owners, most_count):
    counter = jnp.arange(total_count)
    offset_base = jnp.where(counter < most_count, 0, 1 + (counter - most_count) % (owners - 1))
    ordering = jax.random.permutation(jax.random.fold_in(key, 1), total_count)
    rotation = jax.random.randint(jax.random.fold_in(key, 2), (), 0, owners)
    return ((offset_base[ordering] + rotation) % owners).astype(jnp.int32)


def layout_tables(key):
    owners = SECTORS // SEC_DEV
    new_slot = jax.random.permutation(jax.random.fold_in(key, 11), SECTORS).astype(jnp.int32)
    sector_at = jnp.argsort(new_slot).astype(jnp.int32)
    sender_ids = jnp.arange(SECTORS) // SEC_DEV
    within = jnp.arange(SECTORS) % SEC_DEV
    shift_rows = []
    for op_group in range(OPS // OPS_DEV):
        group_key = jax.random.fold_in(key, 100 + op_group)
        offsets = spread_offsets(group_key, OPS_DEV * SEC_DEV, owners, CAP).reshape(OPS_DEV, SEC_DEV)
        owner_order = jax.random.permutation(jax.random.fold_in(group_key, 3), owners)
        local_perms = jax.vmap(lambda sub_key: jax.random.permutation(sub_key, SEC_DEV))(jax.random.split(jax.random.fold_in(group_key, 4), OPS_DEV))
        dest_owner = (owner_order[sender_ids][None, :] + offsets[:, within]) % owners
        dest_slot = dest_owner * SEC_DEV + local_perms[:, within]
        shift_rows.append(sector_at[dest_slot])
    shift_map = jnp.concatenate(shift_rows, axis=0).astype(jnp.int32)
    env_key = jax.random.fold_in(key, 200)
    env_offsets = spread_offsets(env_key, SEC_DEV * ENV_K, owners, ECAP).reshape(SEC_DEV, ENV_K)
    env_order = jax.random.permutation(jax.random.fold_in(env_key, 3), owners)
    source_owner = (env_order[sender_ids][:, None] + env_offsets[within]) % owners
    source_local = jax.random.randint(jax.random.fold_in(env_key, 4), (SECTORS, ENV_K), 0, SEC_DEV)
    by_slot = source_owner * SEC_DEV + source_local
    env_src = by_slot[new_slot].astype(jnp.int32)
    return (shift_map, new_slot, env_src)


def draw_shift_map(key, part):
    return layout_tables(key)[0]


def draw_new_slot(key, part):
    return layout_tables(key)[1]


def draw_env_src(key, part):
    return layout_tables(key)[2]


def levels(rng, dims, cuts, low, high):
    level = 1.0
    for position, shards_of in cuts:
        draws = jax.random.uniform(jax.random.fold_in(jax.random.fold_in(rng, 6), position), (shards_of,), jnp.float32, low / len(cuts), high / len(cuts))
        level = level * jnp.repeat(jnp.exp(draws), dims[position] // shards_of).reshape((-1,) + (1,) * (len(dims) - 1 - position))
    return level


def centred(rng, extent, spread, limit, shards=(), kind=jnp.bfloat16):
    entries = jax.random.normal(rng, extent, jnp.float32) * spread
    if len(shards) > 0:
        entries = levels(rng, extent, shards, -0.22, 0.18) * entries
    return jnp.clip(entries, min=-limit, max=limit).astype(kind)


def setup_inputs(seed: int = 0, part: int = 0) -> dict:
    splits = jax.random.split(jax.random.key(seed), 8)
    part_splits = jax.random.split(jax.random.fold_in(splits[7], part), 8)
    return {
        "ground_state": centred(part_splits[0], (SECTORS, DIM, DIM), 1.0, 6.0, ((0, 4), (1, 2))),
        "op_matrices": centred(part_splits[1], (OPS, DIM, DIM), DIM ** -0.5, 0.25, ((0, 2),)),
        "shift_map": draw_shift_map(jax.random.fold_in(jax.random.fold_in(splits[7], part), 71), part),
        "new_slot": draw_new_slot(jax.random.fold_in(jax.random.fold_in(splits[7], part), 71), part),
        "env_ground": centred(part_splits[4], (SECTORS, DIM, DIM), DIM ** -0.5, 0.25, ((0, 4), (1, 2))),
        "env_src": draw_env_src(jax.random.fold_in(jax.random.fold_in(splits[7], part), 71), part),
        "env_coef": jnp.clip(jax.random.uniform(part_splits[6], (SECTORS, ENV_K), jnp.float32, 0.3, 1.0), 0.3, 1.0),
    }


def reference(ground_state, op_matrices, shift_map, new_slot, env_ground, env_src, env_coef):
    sector_at = jnp.argsort(new_slot).astype(jnp.int32)
    dest_slot = new_slot[shift_map].astype(jnp.int32)
    mixed = jnp.zeros((SECTORS, DIM, DIM), jnp.float32)
    for term_index in range(ENV_K):
        chosen = env_ground[env_src[:, term_index]].astype(jnp.float32)
        mixed = mixed + env_coef[:, term_index][:, None, None] * chosen
    env_slot = mixed.astype(jnp.bfloat16)[sector_at].astype(jnp.float32)
    state_wide = ground_state.astype(jnp.float32)

    def apply_operator(inputs):
        matrix, dest_row = inputs
        products = jnp.einsum('srd,de->sre', state_wide, matrix.astype(jnp.float32)).astype(jnp.bfloat16)
        slot_source = jnp.argsort(dest_row).astype(jnp.int32)
        new_blocks = products[slot_source].astype(jnp.float32)
        return jnp.einsum('jrd,jde->jre', new_blocks, env_slot).astype(jnp.bfloat16)

    return lax.map(apply_operator, (op_matrices, dest_slot))
```

```python
import functools

import jax
import jax.numpy as jnp
from jax import lax
from jax.experimental import pallas as pl
from jax.experimental.pallas import tpu as pltpu
from jax.sharding import PartitionSpec as P

ANY = pl.BlockSpec(memory_space=pl.ANY)
SMEM = pl.BlockSpec(memory_space=pltpu.SMEM)
VMEM = pl.BlockSpec(memory_space=pltpu.VMEM)
BF16 = jnp.bfloat16
LIMIT = 40 << 20


def mix_kernel(dims, picks, places, rows_at, ints, coef, *refs):
    ops, sectors, sec_dev, terms = dims
    count = len(picks)
    sources, refs = refs[:count], refs[count:]
    other = None
    if rows_at is not None:
        other, refs = refs[0], refs[1:]
    outs, (inverse, held, sems) = refs[: len(places)], refs[len(places) :]
    slot_at = ops * sectors
    src_at = slot_at + sectors
    pos_at = src_at + sectors * terms
    busy = ints[pos_at + 2] == 1

    def compute():
        def invert(t, carry):
            inverse[ints[slot_at + t]] = t
            return carry

        lax.fori_loop(0, sectors, invert, 0)

        def copies(place, i, side, act):
            owner = ints[pos_at + place]
            t = inverse[owner * sec_dev + i]
            for k in range(terms):
                source = ints[src_at + t * terms + k]
                if count == 1:
                    act(pltpu.make_async_copy(sources[0].at[source], held.at[side, k], sems.at[side, k]))
                    continue
                code = ints[pos_at + 16 + source // sec_dev]
                for q in range(count):

                    @pl.when(code == q)
                    def _(q=q, k=k, source=source):
                        src = sources[q].at[source % sec_dev]
                        if picks[q] is not None:
                            src = src.at[pl.ds(picks[q], held.shape[2])]
                        act(pltpu.make_async_copy(src, held.at[side, k], sems.at[side, k]))

        steps = [(n, place) for n, place in enumerate(places)]
        for n, place in steps:
            copies(place, 0, 0, lambda c: c.start())

            def step(i, carry, n=n, place=place):
                side = lax.rem(i, 2)

                @pl.when(i + 1 < sec_dev)
                def _():
                    copies(place, i + 1, 1 - side, lambda c: c.start())

                for k in range(terms):
                    pltpu.make_async_copy(held.at[side, k], held.at[side, k], sems.at[side, k]).wait()
                t = inverse[ints[pos_at + place] * sec_dev + i]
                height = min(32, held.shape[2])
                for r in range(0, held.shape[2], height):
                    total = coef[t * terms] * held[side, 0, r : r + height].astype(jnp.float32)
                    for k in range(1, terms):
                        total += coef[t * terms + k] * held[side, k, r : r + height].astype(jnp.float32)
                    outs[n][i, r : r + height] = total.astype(BF16)
                return carry

            lax.fori_loop(0, sec_dev, step, 0)

    if other is None:
        compute()
        return
    pl.when(busy)(compute)

    @pl.when(jnp.logical_not(busy))
    def _():
        copy = pltpu.make_async_copy(other.at[rows_at], outs[0], sems.at[0, 0])
        copy.start()
        copy.wait()


def mix(dims, ints, coef, sources, picks, places, height, other=None, rows_at=None):
    ops, sectors, sec_dev, terms = dims
    columns = sources[0].shape[-1]
    block = jax.ShapeDtypeStruct((sec_dev, height, columns), BF16)
    args = [ints, coef, *sources] + ([] if other is None else [other])
    return pl.pallas_call(
        functools.partial(mix_kernel, dims, picks, places, rows_at),
        out_shape=[block] * len(places),
        in_specs=[SMEM, SMEM] + [ANY] * (len(args) - 2),
        out_specs=[VMEM] * len(places),
        scratch_shapes=[
            pltpu.SMEM((sectors,), jnp.int32),
            pltpu.VMEM((2, terms, height, columns), BF16),
            pltpu.SemaphoreType.DMA((2, terms)),
        ],
        compiler_params=pltpu.CompilerParams(vmem_limit_bytes=LIMIT),
        cost_estimate=pl.CostEstimate(
            flops=2 * terms * len(places) * sec_dev * height * columns,
            bytes_accessed=2 * (terms + 1) * len(places) * sec_dev * height * columns,
            transcendentals=0,
        ),
        name="mix",
    )(*args)


def pair_kernel(dims, ops_dev, counts, pieces, first, ints, where, *refs):
    ops, sectors, sec_dev, terms = dims
    grounds, refs = refs[: len(counts)], refs[len(counts) :]
    op_ref, refs = refs[0], refs[1:]
    env_refs, refs = refs[:pieces], refs[pieces:]
    if not first:
        refs = refs[1:]
    out_ref, found, env, ground, result, env_sem, ground_sem, out_sem = refs
    slot_at = ops * sectors
    pos_at = slot_at + sectors + sectors * terms
    me = ints[pos_at]
    op_base = ints[pos_at + 3] * ops_dev
    env_copies = []
    for n in range(pieces):
        start = pl.multiple_of(where[len(counts) + n], 64)
        env_copies.append(
            pltpu.make_async_copy(env_refs[n], env.at[:, pl.ds(start, env_refs[n].shape[1])], env_sem.at[n])
        )
        env_copies[-1].start()

    def search(n, total):
        base = where[n]

        def candidate(s, total):
            for o in range(ops_dev):
                slot = ints[slot_at + ints[(op_base + o) * sectors + base + s]]
                local = slot - me * sec_dev
                mine = jnp.logical_and(local >= 0, local < sec_dev)
                found[0, total] = n
                found[1, total] = s
                found[2, total] = o
                found[3, total] = local
                total = total + mine.astype(jnp.int32)
            return total

        return lax.fori_loop(0, jnp.where(base >= 0, counts[n], 0), candidate, total)

    total = jnp.int32(0)
    for n in range(len(counts)):
        total = search(n, total)

    def fetch(i, side):
        for n in range(len(counts)):

            @pl.when(found[0, i] == n)
            def _(n=n):
                pltpu.make_async_copy(grounds[n].at[found[1, i]], ground.at[side], ground_sem.at[side]).start()

    @pl.when(total > 0)
    def _():
        fetch(0, 0)

    for copy in env_copies:
        copy.wait()

    def step(i, carry):
        side = lax.rem(i, 2)

        @pl.when(i + 1 < total)
        def _():
            fetch(i + 1, 1 - side)

        pltpu.make_async_copy(ground.at[side], ground.at[side], ground_sem.at[side]).wait()
        o, local = found[2, i], found[3, i]
        product = jnp.dot(ground[side], op_ref[o], preferred_element_type=jnp.float32).astype(BF16)
        grown = jnp.dot(product, env[local], preferred_element_type=jnp.float32).astype(BF16)

        @pl.when(i >= 2)
        def _():
            pltpu.make_async_copy(result.at[side], result.at[side], out_sem.at[side]).wait()

        result[side] = grown
        pltpu.make_async_copy(result.at[side], out_ref.at[o, local], out_sem.at[side]).start()
        return carry

    lax.fori_loop(0, total, step, 0)
    for back in (1, 2):

        @pl.when(total >= back)
        def _(back=back):
            side = lax.rem(total - back, 2)
            pltpu.make_async_copy(result.at[side], result.at[side], out_sem.at[side]).wait()


def pairs(dims, ints, where, grounds, op_matrices, env_pieces, out):
    ops, sectors, sec_dev, terms = dims
    ops_dev = op_matrices.shape[0]
    rows, columns = grounds[0].shape[1:]
    counts = [g.shape[0] for g in grounds]
    shape = jax.ShapeDtypeStruct((ops_dev, sec_dev, rows, columns), BF16)
    args = [ints, where, *grounds, op_matrices, *env_pieces] + ([] if out is None else [out])
    work = max(1, sum(counts) * ops_dev * sec_dev // sectors)
    return pl.pallas_call(
        functools.partial(pair_kernel, dims, ops_dev, counts, len(env_pieces), out is None),
        out_shape=shape,
        in_specs=[SMEM, SMEM] + [ANY] * len(grounds) + [VMEM] + [ANY] * (len(args) - 3 - len(grounds)),
        out_specs=ANY,
        scratch_shapes=[
            pltpu.SMEM((4, sum(counts) * ops_dev + 8), jnp.int32),
            pltpu.VMEM((sec_dev, columns, columns), BF16),
            pltpu.VMEM((2, rows, columns), BF16),
            pltpu.VMEM((2, rows, columns), BF16),
            pltpu.SemaphoreType.DMA((len(env_pieces),)),
            pltpu.SemaphoreType.DMA((2,)),
            pltpu.SemaphoreType.DMA((2,)),
        ],
        input_output_aliases={} if out is None else {len(args) - 1: 0},
        compiler_params=pltpu.CompilerParams(vmem_limit_bytes=LIMIT),
        cost_estimate=pl.CostEstimate(
            flops=4 * work * rows * columns * columns,
            bytes_accessed=2 * (2 * work * rows * columns + (ops_dev + sec_dev) * columns * columns),
            transcendentals=0,
        ),
        name="pairs",
    )(*args)


def pack(shift_map, new_slot, env_src, position):
    return jnp.concatenate(
        [shift_map.reshape(-1), new_slot, env_src.reshape(-1), jnp.stack(position).astype(jnp.int32)]
    )


def whole_gather(ground_state, op_matrices, shift_map, new_slot, env_ground, env_src, env_coef):
    owner = lax.axis_index("sec")
    group = lax.axis_index("op")
    halves = lax.axis_size("op")
    sec_dev, rows, columns = ground_state.shape
    ops, sectors = shift_map.shape
    dims = (ops, sectors, sec_dev, env_src.shape[1])
    zero = jnp.zeros((), jnp.int32)
    ints = pack(shift_map, new_slot, env_src, [owner, zero, zero + 1, group])

    def gather(blocks):
        part = rows // halves
        mine = lax.dynamic_slice_in_dim(blocks, group * part, part, 1)
        whole = lax.all_gather(lax.all_gather(mine, "sec", axis=0, tiled=True), "op", axis=1, tiled=True)
        return whole

    env_all = gather(env_ground)
    (env_new,) = mix(dims, ints, env_coef.reshape(-1), [env_all], [None], [0], rows)
    env_rows = lax.all_gather(env_new, "blk", axis=1, tiled=True)
    where = jnp.zeros((2,), jnp.int32)
    return pairs(dims, ints, where, [gather(ground_state)], op_matrices, [env_rows], None)


def line_of_four(ground_state, op_matrices, shift_map, new_slot, env_ground, env_src, env_coef):
    owner = lax.axis_index("sec")
    group = lax.axis_index("op")
    row_half = lax.axis_index("blk")
    sec_dev, rows, columns = ground_state.shape
    ops, sectors = shift_map.shape
    dims = (ops, sectors, sec_dev, env_src.shape[1])
    half = rows // 2
    spot = jnp.where(group == 0, owner, 3 - owner)

    def stream(steps):
        up = [(2 * a, 2 * a + 2) for a in steps]
        down = [(2 * (3 - a) + 1, 2 * (2 - a) + 1) for a in steps]
        return lambda block: lax.ppermute(block, ("sec", "op"), up + down)

    def swap(block):
        return lax.ppermute(block, "op", [(0, 1), (1, 0)])

    def across(block):
        pairs_of = []
        for z in range(4):
            lead = 0 if z >= 2 else 1
            for x in range(2):
                pairs_of.append(((z * 2 + x) * 2 + lead, (z * 2 + 1 - x) * 2 + 1 - lead))
        return lax.ppermute(block, ("sec", "blk", "op"), pairs_of)

    every, middle, late, last = stream([0, 1, 2]), stream([1]), stream([1, 2]), stream([2])
    ground_half = ground_state.reshape(2, sec_dev, half, columns)
    env_half = env_ground.reshape(sec_dev, 2, half, columns)
    is_two = spot == 2
    ahead = jnp.where(group == 0, owner + 1, owner - 1)
    code = [jnp.where(group == 0, w, 3 - w) for w in range(4)]
    position = [owner, ahead, is_two, group] + [jnp.zeros((), jnp.int32)] * 12 + code
    coef = env_coef.reshape(-1)

    sent0 = [jnp.where(is_two, ground_half[h], env_half[:, h]) for h in range(2)]
    got0 = [every(sent0[h]) for h in range(2)]
    got2 = [middle(got0[h]) for h in range(2)]
    swapped0 = [swap(got0[h]) for h in range(2)]
    ints = pack(shift_map, new_slot, env_src, position)
    sent4, env_new = [], []
    for h in range(2):
        passed, made = mix(
            dims, ints, coef, [got2[h], got0[h], env_ground, swapped0[h]], [None, None, h * half, None], [1, 0],
            half, ground_half, h,
        )
        sent4.append(passed)
        env_new.append(made)
    got4 = [every(sent4[h]) for h in range(2)]
    got6 = [late(got4[h]) for h in range(2)]
    got8 = [last(got6[h]) for h in range(2)]
    swapped4 = [swap(got4[h]) for h in range(2)]
    swapped6 = [swap(got6[h]) for h in range(2)]
    swapped8 = [swap(got8[h]) for h in range(2)]
    env_pieces, env_starts = [], []
    lead = spot >= 2
    for h in range(2):
        mine = jnp.where(is_two, env_new[h], got4[h])
        received = across(mine)
        kept = jnp.where(lead, mine, received)
        env_pieces += [kept, swap(kept)]
        own, far = row_half * rows + h * half, (1 - row_half) * rows + h * half
        env_starts += [jnp.where(lead, own, far), jnp.where(lead, far, own)]

    step = jnp.where(group == 0, -1, 1)

    def base(own_hops, h):
        hops = jnp.asarray(own_hops, jnp.int32)
        own = jnp.where(hops[spot] > 0, (owner + step * hops[spot]) * sec_dev + h * (sec_dev // 2), -1)
        other = hops[3 - spot]
        theirs = jnp.where(other > 0, (owner - step * other) * sec_dev + h * (sec_dev // 2), -1)
        return [own, theirs]

    def blocks(block):
        return block.reshape(sec_dev // 2, rows, columns)

    def stage(out, arrays, bases):
        where = jnp.stack([jnp.asarray(b, jnp.int32) for b in bases + env_starts])
        return pairs(dims, ints, where, arrays, op_matrices, env_pieces, out)

    arrays, bases = [ground_state], [owner * sec_dev]
    for h in range(2):
        arrays += [blocks(got0[h]), blocks(swapped0[h]), blocks(got4[h]), blocks(swapped4[h])]
        bases += base([0, 0, 0, 1], h) + base([0, 1, 1, 0], h)
    out = stage(None, arrays, bases)
    arrays, bases = [], []
    for h in range(2):
        arrays += [blocks(got6[h]), blocks(swapped6[h])]
        bases += base([0, 0, 2, 2], h)
    out = stage(out, arrays, bases)
    for h in range(2):
        out = stage(out, [blocks(got8[h]), blocks(swapped8[h])], base([0, 0, 0, 3], h))
    return out


def solution(mesh):
    four = mesh.shape["sec"] == 4 and mesh.shape["blk"] == 2 and mesh.shape["op"] == 2
    return jax.shard_map(
        line_of_four if four else whole_gather,
        mesh=mesh,
        in_specs=(
            P(("grp", "sec"), "blk", None),
            P(("grp", "op"), None, None),
            P("grp", None),
            P("grp"),
            P(("grp", "sec"), "blk", None),
            P("grp", None),
            P("grp", None),
        ),
        out_specs=P(("grp", "op"), "sec", "blk", None),
        check_vma=False,
    )
```

```python
import functools

import jax
import jax.numpy as jnp
from jax import lax
from jax.experimental import pallas as pl
from jax.experimental.pallas import tpu as pltpu
from jax.sharding import PartitionSpec as P

ANY = pl.BlockSpec(memory_space=pl.ANY)
HBM = pl.BlockSpec(memory_space=pltpu.HBM)
SMEM = pl.BlockSpec(memory_space=pltpu.SMEM)
VMEM = pl.BlockSpec(memory_space=pltpu.VMEM)
BF16 = jnp.bfloat16
LIMIT = 40 << 20
LARGE = 60 << 20
MEDIUM = 28 << 20


def mix_kernel(dims, picks, places, rows_at, ints, coef, *refs):
    ops, sectors, sec_dev, terms = dims
    count = len(picks)
    sources, refs = refs[:count], refs[count:]
    other = None
    if rows_at is not None:
        other, refs = refs[0], refs[1:]
    outs, (inverse, held, sems) = refs[: len(places)], refs[len(places) :]
    slot_at = ops * sectors
    src_at = slot_at + sectors
    pos_at = src_at + sectors * terms
    busy = ints[pos_at + 2] == 1

    def compute():
        def invert(t, carry):
            inverse[ints[slot_at + t]] = t
            return carry

        lax.fori_loop(0, sectors, invert, 0)

        def copies(place, i, side, act):
            owner = ints[pos_at + place]
            t = inverse[owner * sec_dev + i]
            for k in range(terms):
                source = ints[src_at + t * terms + k]
                if count == 1:
                    act(pltpu.make_async_copy(sources[0].at[source], held.at[side, k], sems.at[side, k]))
                    continue
                code = ints[pos_at + 16 + source // sec_dev]
                for q in range(count):

                    @pl.when(code == q)
                    def _(q=q, k=k, source=source):
                        src = sources[q].at[source % sec_dev]
                        if picks[q] is not None:
                            src = src.at[pl.ds(picks[q], held.shape[2])]
                        act(pltpu.make_async_copy(src, held.at[side, k], sems.at[side, k]))

        steps = [(n, place) for n, place in enumerate(places)]
        for n, place in steps:
            copies(place, 0, 0, lambda c: c.start())

            def step(i, carry, n=n, place=place):
                side = lax.rem(i, 2)

                @pl.when(i + 1 < sec_dev)
                def _():
                    copies(place, i + 1, 1 - side, lambda c: c.start())

                for k in range(terms):
                    pltpu.make_async_copy(held.at[side, k], held.at[side, k], sems.at[side, k]).wait()
                t = inverse[ints[pos_at + place] * sec_dev + i]
                height = min(32, held.shape[2])
                for r in range(0, held.shape[2], height):
                    total = coef[t * terms] * held[side, 0, r : r + height].astype(jnp.float32)
                    for k in range(1, terms):
                        total += coef[t * terms + k] * held[side, k, r : r + height].astype(jnp.float32)
                    outs[n][i, r : r + height] = total.astype(BF16)
                return carry

            lax.fori_loop(0, sec_dev, step, 0)

    if other is None:
        compute()
        return
    pl.when(busy)(compute)

    @pl.when(jnp.logical_not(busy))
    def _():
        copy = pltpu.make_async_copy(other.at[rows_at], outs[0], sems.at[0, 0])
        copy.start()
        copy.wait()


def mix(dims, ints, coef, sources, picks, places, height, other=None, rows_at=None):
    ops, sectors, sec_dev, terms = dims
    columns = sources[0].shape[-1]
    block = jax.ShapeDtypeStruct((sec_dev, height, columns), BF16)
    args = [ints, coef, *sources] + ([] if other is None else [other])
    return pl.pallas_call(
        functools.partial(mix_kernel, dims, picks, places, rows_at),
        out_shape=[block] * len(places),
        in_specs=[SMEM, SMEM] + [ANY] * (len(args) - 2),
        out_specs=[VMEM] * len(places),
        scratch_shapes=[
            pltpu.SMEM((sectors,), jnp.int32),
            pltpu.VMEM((2, terms, height, columns), BF16),
            pltpu.SemaphoreType.DMA((2, terms)),
        ],
        compiler_params=pltpu.CompilerParams(vmem_limit_bytes=LIMIT),
        cost_estimate=pl.CostEstimate(
            flops=2 * terms * len(places) * sec_dev * height * columns,
            bytes_accessed=2 * (terms + 1) * len(places) * sec_dev * height * columns,
            transcendentals=0,
        ),
        name="mix",
    )(*args)


def pair_kernel(dims, ops_dev, counts, pieces, first, ints, where, *refs):
    ops, sectors, sec_dev, terms = dims
    grounds, refs = refs[: len(counts)], refs[len(counts) :]
    op_ref, refs = refs[0], refs[1:]
    env_refs, refs = refs[:pieces], refs[pieces:]
    if not first:
        refs = refs[1:]
    out_ref, found, env, ground, result, env_sem, ground_sem, out_sem = refs
    slot_at = ops * sectors
    pos_at = slot_at + sectors + sectors * terms
    me = ints[pos_at]
    op_base = ints[pos_at + 3] * ops_dev
    env_copies = []
    for n in range(pieces):
        start = pl.multiple_of(where[len(counts) + n], 64)
        env_copies.append(
            pltpu.make_async_copy(env_refs[n], env.at[:, pl.ds(start, env_refs[n].shape[1])], env_sem.at[n])
        )
        env_copies[-1].start()

    def search(n, total):
        base = where[n]

        def candidate(s, total):
            for o in range(ops_dev):
                slot = ints[slot_at + ints[(op_base + o) * sectors + base + s]]
                local = slot - me * sec_dev
                mine = jnp.logical_and(local >= 0, local < sec_dev)
                found[0, total] = n
                found[1, total] = s
                found[2, total] = o
                found[3, total] = local
                total = total + mine.astype(jnp.int32)
            return total

        return lax.fori_loop(0, jnp.where(base >= 0, counts[n], 0), candidate, total)

    total = jnp.int32(0)
    for n in range(len(counts)):
        total = search(n, total)

    def fetch(i, side):
        for n in range(len(counts)):

            @pl.when(found[0, i] == n)
            def _(n=n):
                pltpu.make_async_copy(grounds[n].at[found[1, i]], ground.at[side], ground_sem.at[side]).start()

    @pl.when(total > 0)
    def _():
        fetch(0, 0)

    for copy in env_copies:
        copy.wait()

    def step(i, carry):
        side = lax.rem(i, 2)

        @pl.when(i + 1 < total)
        def _():
            fetch(i + 1, 1 - side)

        pltpu.make_async_copy(ground.at[side], ground.at[side], ground_sem.at[side]).wait()
        o, local = found[2, i], found[3, i]
        product = jnp.dot(ground[side], op_ref[o], preferred_element_type=jnp.float32).astype(BF16)
        grown = jnp.dot(product, env[local], preferred_element_type=jnp.float32).astype(BF16)

        @pl.when(i >= 2)
        def _():
            pltpu.make_async_copy(result.at[side], result.at[side], out_sem.at[side]).wait()

        result[side] = grown
        pltpu.make_async_copy(result.at[side], out_ref.at[o, local], out_sem.at[side]).start()
        return carry

    lax.fori_loop(0, total, step, 0)
    for back in (1, 2):

        @pl.when(total >= back)
        def _(back=back):
            side = lax.rem(total - back, 2)
            pltpu.make_async_copy(result.at[side], result.at[side], out_sem.at[side]).wait()


def pairs(dims, ints, where, grounds, op_matrices, env_pieces, out):
    ops, sectors, sec_dev, terms = dims
    ops_dev = op_matrices.shape[0]
    rows, columns = grounds[0].shape[1:]
    counts = [g.shape[0] for g in grounds]
    shape = jax.ShapeDtypeStruct((ops_dev, sec_dev, rows, columns), BF16)
    args = [ints, where, *grounds, op_matrices, *env_pieces] + ([] if out is None else [out])
    work = max(1, sum(counts) * ops_dev * sec_dev // sectors)
    return pl.pallas_call(
        functools.partial(pair_kernel, dims, ops_dev, counts, len(env_pieces), out is None),
        out_shape=shape,
        in_specs=[SMEM, SMEM] + [ANY] * len(grounds) + [VMEM] + [ANY] * (len(args) - 3 - len(grounds)),
        out_specs=ANY,
        scratch_shapes=[
            pltpu.SMEM((4, sum(counts) * ops_dev + 8), jnp.int32),
            pltpu.VMEM((sec_dev, columns, columns), BF16),
            pltpu.VMEM((2, rows, columns), BF16),
            pltpu.VMEM((2, rows, columns), BF16),
            pltpu.SemaphoreType.DMA((len(env_pieces),)),
            pltpu.SemaphoreType.DMA((2,)),
            pltpu.SemaphoreType.DMA((2,)),
        ],
        input_output_aliases={} if out is None else {len(args) - 1: 0},
        compiler_params=pltpu.CompilerParams(vmem_limit_bytes=LIMIT),
        cost_estimate=pl.CostEstimate(
            flops=4 * work * rows * columns * columns,
            bytes_accessed=2 * (2 * work * rows * columns + (ops_dev + sec_dev) * columns * columns),
            transcendentals=0,
        ),
        name="pairs",
    )(*args)


def pack(shift_map, new_slot, env_src, position):
    return jnp.concatenate(
        [shift_map.reshape(-1), new_slot, env_src.reshape(-1), jnp.stack(position).astype(jnp.int32)]
    )


def whole_gather(ground_state, op_matrices, shift_map, new_slot, env_ground, env_src, env_coef):
    owner = lax.axis_index("sec")
    group = lax.axis_index("op")
    halves = lax.axis_size("op")
    sec_dev, rows, columns = ground_state.shape
    ops, sectors = shift_map.shape
    dims = (ops, sectors, sec_dev, env_src.shape[1])
    zero = jnp.zeros((), jnp.int32)
    ints = pack(shift_map, new_slot, env_src, [owner, zero, zero + 1, group])

    def gather(blocks):
        part = rows // halves
        mine = lax.dynamic_slice_in_dim(blocks, group * part, part, 1)
        whole = lax.all_gather(lax.all_gather(mine, "sec", axis=0, tiled=True), "op", axis=1, tiled=True)
        return whole

    env_all = gather(env_ground)
    (env_new,) = mix(dims, ints, env_coef.reshape(-1), [env_all], [None], [0], rows)
    env_rows = lax.all_gather(env_new, "blk", axis=1, tiled=True)
    where = jnp.zeros((2,), jnp.int32)
    return pairs(dims, ints, where, [gather(ground_state)], op_matrices, [env_rows], None)


DEPTH = 4
GROW_COST = 40 * 10**9
MIX_WIDTH = 8
LIST = 16


def device_place():
    owner, core = lax.axis_index("sec"), lax.axis_index("op")
    return owner, core, jnp.where(core == 0, owner, 3 - owner)


def by_spot(spot, values):
    result = jnp.int32(values[0])
    for n in range(1, 4):
        result = jnp.where(spot == n, values[n], result)
    return result


def head_kernel(env, ground, first, second, sems):
    _, _, spot = device_place()
    half = env.shape[1] // 2

    def send(sources):
        copies = [pltpu.make_async_copy(sources[h], (first, second)[h], sems.at[h]) for h in range(2)]
        for copy in copies:
            copy.start()
        for copy in copies:
            copy.wait()

    pl.when(spot == 2)(lambda: send([ground.at[h] for h in range(2)]))
    pl.when(spot != 2)(lambda: send([env.at[:, pl.ds(h * half, half)] for h in range(2)]))


def head(env_ground, ground_half):
    sec_dev, rows, columns = env_ground.shape
    block = jax.ShapeDtypeStruct((sec_dev, rows // 2, columns), BF16)
    return pl.pallas_call(
        head_kernel,
        out_shape=[block, block],
        in_specs=[HBM, HBM],
        out_specs=[VMEM, VMEM],
        scratch_shapes=[pltpu.SemaphoreType.DMA((2,))],
        compiler_params=pltpu.CompilerParams(vmem_limit_bytes=LARGE),
        cost_estimate=pl.CostEstimate(flops=0, bytes_accessed=4 * sec_dev * rows * columns, transcendentals=0),
        name="head",
    )(env_ground, ground_half)


def tables_kernel(dims, ops_dev, shift, slot, src, table, inverse):
    ops, sectors, sec_dev, terms = dims
    owner, core, _ = device_place()
    ahead = jnp.where(core == 0, jnp.minimum(owner + 1, 3), jnp.maximum(owner - 1, 0))

    def invert(t, carry):
        inverse[slot[t]] = t
        return carry

    lax.fori_loop(0, sectors, invert, 0)

    def terms_of(i, carry):
        place = jnp.where(i < sec_dev, ahead * sec_dev + i, owner * sec_dev + i - sec_dev)
        t = inverse[place]
        table[i * MIX_WIDTH] = t
        for k in range(terms):
            source = src[k, t]
            from_owner = source // sec_dev
            table[i * MIX_WIDTH + 1 + 2 * k] = jnp.where(core == 0, from_owner, 3 - from_owner)
            table[i * MIX_WIDTH + 2 + 2 * k] = source - from_owner * sec_dev
        return carry

    lax.fori_loop(0, 2 * sec_dev, terms_of, 0)
    count_at = 2 * sec_dev * MIX_WIDTH
    list_at = count_at + 8
    width = sec_dev // 2

    def pairs_of(n, carry):
        total = jnp.int32(0)
        for s in range(width):
            for o in range(ops_dev):
                local = slot[shift[core * ops_dev + o, n * width + s]] - owner * sec_dev
                table[list_at + n * LIST + total] = (s * ops_dev + o) * sec_dev + local
                total = total + jnp.logical_and(local >= 0, local < sec_dev).astype(jnp.int32)
        table[count_at + n] = total
        return carry

    lax.fori_loop(0, sectors // width, pairs_of, 0)


def tables(dims, ops_dev, shift_map, new_slot, env_src):
    ops, sectors, sec_dev, terms = dims
    return pl.pallas_call(
        functools.partial(tables_kernel, dims, ops_dev),
        out_shape=jax.ShapeDtypeStruct((2 * sec_dev * MIX_WIDTH + 8 + 8 * LIST,), jnp.int32),
        in_specs=[SMEM, SMEM, SMEM],
        out_specs=SMEM,
        scratch_shapes=[pltpu.SMEM((sectors,), jnp.int32)],
        cost_estimate=pl.CostEstimate(flops=10000, bytes_accessed=4000, transcendentals=0),
        name="tables",
    )(shift_map, new_slot, env_src)


def blend_kernel(dims, which, table, coef, second, first, env, other, ground, passed, made, held, sems):
    ops, sectors, sec_dev, terms = dims
    _, _, spot = device_place()
    height = held.shape[2]
    sources = [second, first, env.at[:, pl.ds(which * height, height)], other]

    @pl.when(spot == 2)
    def _():
        def fetch(i, carry):
            for k in range(terms):
                code, block = table[i * MIX_WIDTH + 1 + 2 * k], table[i * MIX_WIDTH + 2 + 2 * k]
                for q in range(4):

                    @pl.when(code == q)
                    def _(q=q, k=k, block=block):
                        pltpu.make_async_copy(sources[q].at[block], held.at[i, k], sems.at[i]).start()

            return carry

        lax.fori_loop(0, 2 * sec_dev, fetch, 0)

        def sums(out, lead):
            def one(i, carry):
                at = i + lead
                pltpu.make_async_copy(held.at[at], held.at[at], sems.at[at]).wait()
                t = table[at * MIX_WIDTH]
                weights = [coef[k, t] for k in range(terms)]
                for r in range(0, height, 32):
                    total = weights[0] * held[at, 0, r : r + 32].astype(jnp.float32)
                    for k in range(1, terms):
                        total += weights[k] * held[at, k, r : r + 32].astype(jnp.float32)
                    out[i, r : r + 32] = total.astype(BF16)
                return carry

            lax.fori_loop(0, sec_dev, one, 0)

        sums(passed, 0)
        sums(made, sec_dev)

    @pl.when(spot != 2)
    def _():
        copy = pltpu.make_async_copy(ground.at[which], passed, sems.at[0])
        copy.start()
        copy.wait()


def blend(dims, which, table, coef, second, first, env_ground, other, ground_half):
    ops, sectors, sec_dev, terms = dims
    block = jax.ShapeDtypeStruct(first.shape, BF16)
    _, height, columns = first.shape
    return pl.pallas_call(
        functools.partial(blend_kernel, dims, which),
        out_shape=[block, block],
        in_specs=[SMEM, SMEM] + [HBM] * 5,
        out_specs=[VMEM, VMEM],
        scratch_shapes=[
            pltpu.VMEM((2 * sec_dev, terms, height, columns), BF16),
            pltpu.SemaphoreType.DMA((2 * sec_dev,)),
        ],
        compiler_params=pltpu.CompilerParams(vmem_limit_bytes=MEDIUM),
        cost_estimate=pl.CostEstimate(
            flops=4 * terms * sec_dev * height * columns,
            bytes_accessed=4 * (terms + 1) * sec_dev * height * columns,
            transcendentals=0,
        ),
        name="blend",
    )(table, coef, second, first, env_ground, other, ground_half)


def half_owner(owner, core, spot, hops, h, sibling):
    if hops is None:
        return 2 * owner + h
    n = by_spot(3 - spot if sibling else spot, hops)
    back = jnp.where(core == 0, -1, 1) * (-1 if sibling else 1)
    return jnp.where(n > 0, 2 * (owner + back * n) + h, -1)


def grow_kernel(dims, ops_dev, parts, arrays, table, *refs):
    ops, sectors, sec_dev, terms = dims
    grounds, op_ref, refs = refs[:arrays], refs[arrays], refs[arrays + 1 :]
    owner, core, spot = device_place()
    rows, columns = grounds[0].shape[1:]
    width = sec_dev // 2
    pieces, (out_ref, env, found, ground, result, ground_sem, out_sem, env_sem) = refs[:16], refs[16:]
    count_at = 2 * sec_dev * MIX_WIDTH
    list_at = count_at + 8
    part_of = [half_owner(owner, core, spot, hops, h, sibling) for _, hops, h, sibling, _ in parts]
    for m, (n, _, _, _, lead) in enumerate(parts):

        @pl.when(part_of[m] >= 0)
        def _(m=m, n=n, lead=lead):
            source = grounds[n].at[pl.ds(lead, width)]
            pltpu.make_async_copy(source, ground.at[pl.ds(m * width, width)], ground_sem.at[m]).start()

    env_copies = []
    half = rows // 2
    own = lax.axis_index("blk") * rows
    for n, start in enumerate((own, rows - own, own + half, rows - own + half)):
        target = env.at[:, pl.ds(pl.multiple_of(start, half), half)]
        for q in range(4):

            @pl.when(spot == q)
            def _(n=n, q=q, target=target):
                pltpu.make_async_copy(pieces[4 * n + q], target, env_sem.at[n]).start()

        env_copies.append(pltpu.make_async_copy(target, target, env_sem.at[n]))

    total = jnp.int32(0)
    for m in range(len(parts)):
        part = part_of[m]
        count = jnp.where(part >= 0, table[count_at + jnp.maximum(part, 0)], 0)

        def take(i, carry, total=total, part=part, m=m):
            entry = table[list_at + part * LIST + i]
            rest = entry // sec_dev
            found[0, total + i] = m * width + rest // ops_dev
            found[1, total + i] = lax.rem(rest, ops_dev)
            found[2, total + i] = lax.rem(entry, sec_dev)
            return carry

        lax.fori_loop(0, count, take, 0)
        total = total + count
    for copy in env_copies:
        copy.wait()
    for m in range(len(parts)):

        @pl.when(part_of[m] >= 0)
        def _(m=m):
            here = ground.at[pl.ds(m * width, width)]
            pltpu.make_async_copy(here, here, ground_sem.at[m]).wait()

    def drain(side):
        pltpu.make_async_copy(result.at[side], result.at[side], out_sem.at[side]).wait()

    def step(i, carry):
        side = lax.rem(i, DEPTH)
        o, local = found[1, i], found[2, i]
        product = jnp.dot(ground[found[0, i]], op_ref[o], preferred_element_type=jnp.float32).astype(BF16)
        grown = jnp.dot(product, env[local], preferred_element_type=jnp.float32).astype(BF16)
        pl.when(i >= DEPTH)(lambda: drain(side))
        result[side] = grown
        pltpu.make_async_copy(result.at[side], out_ref.at[o, local], out_sem.at[side]).start()
        return carry

    lax.fori_loop(0, total, step, 0)
    for back in range(1, DEPTH + 1):
        pl.when(total >= back)(lambda back=back: drain(lax.rem(total - back, DEPTH)))


def grow(dims, table, parts, grounds, op_matrices, pieces):
    ops, sectors, sec_dev, terms = dims
    ops_dev = op_matrices.shape[0]
    rows, columns = grounds[0].shape[1:]
    return pl.pallas_call(
        functools.partial(grow_kernel, dims, ops_dev, parts, len(grounds)),
        out_shape=[
            jax.ShapeDtypeStruct((ops_dev, sec_dev, rows, columns), BF16),
            jax.ShapeDtypeStruct((sec_dev, columns, columns), BF16),
        ],
        in_specs=[SMEM] + [ANY] * len(grounds) + [VMEM] + [ANY] * len(pieces),
        out_specs=[ANY, VMEM],
        scratch_shapes=[
            pltpu.SMEM((3, LIST * len(parts)), jnp.int32),
            pltpu.VMEM((sec_dev // 2 * len(parts), rows, columns), BF16),
            pltpu.VMEM((DEPTH, rows, columns), BF16),
            pltpu.SemaphoreType.DMA((len(parts),)),
            pltpu.SemaphoreType.DMA((DEPTH,)),
            pltpu.SemaphoreType.DMA((4,)),
        ],
        compiler_params=pltpu.CompilerParams(vmem_limit_bytes=MEDIUM),
        cost_estimate=pl.CostEstimate(flops=1 << 20, bytes_accessed=1 << 12, transcendentals=0),
        name="grow",
    )(table, *grounds, op_matrices, *pieces)


def finish_kernel(dims, ops_dev, table, own_a, other_a, own_b, other_b, op_ref, env, _, out_ref, found, result, out_sem):
    ops, sectors, sec_dev, terms = dims
    owner, core, spot = device_place()
    count_at = 2 * sec_dev * MIX_WIDTH
    list_at = count_at + 8
    total = jnp.int32(0)
    for h in range(2):
        part = jnp.where(spot == 3, half_owner(owner, core, spot, [0, 0, 0, 3], h, False), -1)
        part = jnp.where(spot == 0, half_owner(owner, core, spot, [0, 0, 0, 3], h, True), part)
        count = jnp.where(part >= 0, table[count_at + jnp.maximum(part, 0)], 0)

        def take(n, carry, part=part, total=total, h=h):
            entry = table[list_at + part * LIST + n]
            rest = entry // sec_dev
            found[0, total + n] = h
            found[1, total + n] = rest // ops_dev
            found[2, total + n] = lax.rem(rest, ops_dev)
            found[3, total + n] = lax.rem(entry, sec_dev)
            return carry

        lax.fori_loop(0, count, take, 0)
        total = total + count

    def drain(side):
        pltpu.make_async_copy(result.at[side], result.at[side], out_sem.at[side]).wait()

    def step(i, carry):
        side = lax.rem(i, DEPTH)
        h, s, o, local = (found[k, i] for k in range(4))
        first = jnp.where(spot == 3, own_a[s], other_a[s])
        second = jnp.where(spot == 3, own_b[s], other_b[s])
        block = jnp.where(h == 0, first, second)
        product = jnp.dot(block, op_ref[o], preferred_element_type=jnp.float32).astype(BF16)
        grown = jnp.dot(product, env[local], preferred_element_type=jnp.float32).astype(BF16)
        pl.when(i >= DEPTH)(lambda: drain(side))
        result[side] = grown
        pltpu.make_async_copy(result.at[side], out_ref.at[o, local], out_sem.at[side]).start()
        return carry

    lax.fori_loop(0, total, step, 0)
    for back in range(1, DEPTH + 1):
        pl.when(total >= back)(lambda back=back: drain(lax.rem(total - back, DEPTH)))


def finish(dims, table, ends, op_matrices, env, out):
    ops, sectors, sec_dev, terms = dims
    ops_dev, _, rows, columns = out.shape
    return pl.pallas_call(
        functools.partial(finish_kernel, dims, ops_dev),
        out_shape=jax.ShapeDtypeStruct(out.shape, BF16),
        in_specs=[SMEM] + [VMEM] * 6 + [ANY],
        out_specs=ANY,
        scratch_shapes=[
            pltpu.SMEM((4, sec_dev * ops_dev), jnp.int32),
            pltpu.VMEM((DEPTH, rows, columns), BF16),
            pltpu.SemaphoreType.DMA((DEPTH,)),
        ],
        input_output_aliases={7: 0},
        compiler_params=pltpu.CompilerParams(vmem_limit_bytes=MEDIUM),
        cost_estimate=pl.CostEstimate(flops=GROW_COST, bytes_accessed=1 << 20, transcendentals=0),
        name="finish",
    )(table, *ends, op_matrices, env, out)


def line_of_four(ground_state, op_matrices, shift_map, new_slot, env_ground, env_src, env_coef):
    sec_dev, rows, columns = ground_state.shape
    ops, sectors = shift_map.shape
    ops_dev = op_matrices.shape[0]
    dims = (ops, sectors, sec_dev, env_src.shape[1])
    half = rows // 2

    def stream(steps):
        up = [(2 * a, 2 * a + 2) for a in steps]
        down = [(2 * (3 - a) + 1, 2 * (2 - a) + 1) for a in steps]
        return lambda block: lax.ppermute(block, ("sec", "op"), up + down)

    def hand(block, spots):
        pairs_of = [(2 * z + core, 2 * z + 1 - core) for spot in spots for z, core in at[spot]]
        return lax.ppermute(block, ("sec", "op"), pairs_of)

    def across(block, spot):
        pairs_of = [((z * 2 + x) * 2 + core, (z * 2 + 1 - x) * 2 + 1 - core) for z, core in at[spot] for x in range(2)]
        return lax.ppermute(block, ("sec", "blk", "op"), pairs_of)

    def after(block, *others):
        return lax.optimization_barrier((block, *others))[0]

    at = [[(0, 0), (3, 1)], [(1, 0), (2, 1)], [(2, 0), (1, 1)], [(3, 0), (0, 1)]]
    every, middle, late, last = stream([0, 1, 2]), stream([1]), stream([1, 2]), stream([2])
    ground_half = ground_state.reshape(2, sec_dev, half, columns)
    both = range(2)

    sent0 = head(env_ground, ground_half)
    got0 = [every(sent0[h]) for h in both]
    got2 = [middle(got0[h]) for h in both]
    swapped0 = [hand(got0[h], [1, 3]) for h in both]
    table = tables(dims, ops_dev, shift_map, new_slot, env_src.T)
    sent4, made = zip(
        *[blend(dims, h, table, env_coef.T, got2[h], got0[h], env_ground, swapped0[h], ground_half) for h in both]
    )
    got4 = [every(sent4[h]) for h in both]
    got6 = [late(got4[h]) for h in both]
    far1 = [across(after(made[0], got2[1]), 2), across(after(made[1], got4[0]), 2)]
    far2 = [across(got4[0], 3), across(got4[1], 3)]
    near1 = [hand(after(made[0], got4[1]), [2]), hand(after(made[1], got4[1]), [2])]
    back1 = [hand(after(far1[0], got4[1]), [1]), hand(after(far1[1], got4[1]), [1])]
    swapped4 = [hand(after(got4[0], got4[1]), [1, 2, 3]), hand(after(got4[1], far2[0]), [1, 2, 3])]
    back2 = [hand(far2[0], [0]), hand(after(far2[1], got6[1]), [0])]
    swapped6 = [hand(after(got6[h], got6[1]), [2, 3]) for h in both]
    got8 = [
        last(after(got6[0], *far1, far2[0], near1[0], back1[0], swapped4[0])),
        last(after(got6[1], *near1, *back1, back2[0], *swapped4)),
    ]
    pieces = []
    for h in both:
        pieces += [swapped4[h], near1[h], made[h], got4[h]]
        pieces += [far2[h], far1[h], back1[h], back2[h]]

    parts = [(0, None, h, False, h * sec_dev // 2) for h in both]
    arrays = [ground_state]

    def hold(mine, theirs, hops, h):
        for block, sibling in ((mine, False), (theirs, True)):
            parts.append((len(arrays), hops, h, sibling, 0))
            arrays.append(block.reshape(sec_dev // 2, rows, columns))

    for h in both:
        hold(got0[h], swapped0[h], [0, 0, 0, 1], h)
        hold(got4[h], swapped4[h], [0, 1, 1, 0], h)
    for h in both:
        hold(got6[h], swapped6[h], [0, 0, 2, 2], h)
    out, env = grow(dims, table, parts, arrays, op_matrices, pieces)
    swapped8 = [hand(after(got8[h], out), [3]) for h in both]
    ends = [block[h].reshape(sec_dev // 2, rows, columns) for h in both for block in (got8, swapped8)]
    return finish(dims, table, ends, op_matrices, env, out)


def solution(mesh):
    four = mesh.shape["sec"] == 4 and mesh.shape["blk"] == 2 and mesh.shape["op"] == 2
    return jax.shard_map(
        line_of_four if four else whole_gather,
        mesh=mesh,
        in_specs=(
            P(("grp", "sec"), "blk", None),
            P(("grp", "op"), None, None),
            P("grp", None),
            P("grp"),
            P(("grp", "sec"), "blk", None),
            P("grp", None),
            P("grp", None),
        ),
        out_specs=P(("grp", "op"), "sec", "blk", None),
        check_vma=False,
    )
```

```python
import functools

import jax
import jax.numpy as jnp
from jax import lax
from jax.experimental import pallas as pl
from jax.experimental.pallas import tpu as pltpu
from jax.sharding import PartitionSpec as P

ANY = pl.BlockSpec(memory_space=pl.ANY)
HBM = pl.BlockSpec(memory_space=pltpu.HBM)
SMEM = pl.BlockSpec(memory_space=pltpu.SMEM)
VMEM = pl.BlockSpec(memory_space=pltpu.VMEM)
BF16 = jnp.bfloat16
LIMIT = 40 << 20
LARGE = 60 << 20
MEDIUM = 28 << 20


def mix_kernel(dims, picks, places, rows_at, ints, coef, *refs):
    ops, sectors, sec_dev, terms = dims
    count = len(picks)
    sources, refs = refs[:count], refs[count:]
    other = None
    if rows_at is not None:
        other, refs = refs[0], refs[1:]
    outs, (inverse, held, sems) = refs[: len(places)], refs[len(places) :]
    slot_at = ops * sectors
    src_at = slot_at + sectors
    pos_at = src_at + sectors * terms
    busy = ints[pos_at + 2] == 1

    def compute():
        def invert(t, carry):
            inverse[ints[slot_at + t]] = t
            return carry

        lax.fori_loop(0, sectors, invert, 0)

        def copies(place, i, side, act):
            owner = ints[pos_at + place]
            t = inverse[owner * sec_dev + i]
            for k in range(terms):
                source = ints[src_at + t * terms + k]
                if count == 1:
                    act(pltpu.make_async_copy(sources[0].at[source], held.at[side, k], sems.at[side, k]))
                    continue
                code = ints[pos_at + 16 + source // sec_dev]
                for q in range(count):

                    @pl.when(code == q)
                    def _(q=q, k=k, source=source):
                        src = sources[q].at[source % sec_dev]
                        if picks[q] is not None:
                            src = src.at[pl.ds(picks[q], held.shape[2])]
                        act(pltpu.make_async_copy(src, held.at[side, k], sems.at[side, k]))

        steps = [(n, place) for n, place in enumerate(places)]
        for n, place in steps:
            copies(place, 0, 0, lambda c: c.start())

            def step(i, carry, n=n, place=place):
                side = lax.rem(i, 2)

                @pl.when(i + 1 < sec_dev)
                def _():
                    copies(place, i + 1, 1 - side, lambda c: c.start())

                for k in range(terms):
                    pltpu.make_async_copy(held.at[side, k], held.at[side, k], sems.at[side, k]).wait()
                t = inverse[ints[pos_at + place] * sec_dev + i]
                height = min(32, held.shape[2])
                for r in range(0, held.shape[2], height):
                    total = coef[t * terms] * held[side, 0, r : r + height].astype(jnp.float32)
                    for k in range(1, terms):
                        total += coef[t * terms + k] * held[side, k, r : r + height].astype(jnp.float32)
                    outs[n][i, r : r + height] = total.astype(BF16)
                return carry

            lax.fori_loop(0, sec_dev, step, 0)

    if other is None:
        compute()
        return
    pl.when(busy)(compute)

    @pl.when(jnp.logical_not(busy))
    def _():
        copy = pltpu.make_async_copy(other.at[rows_at], outs[0], sems.at[0, 0])
        copy.start()
        copy.wait()


def mix(dims, ints, coef, sources, picks, places, height, other=None, rows_at=None):
    ops, sectors, sec_dev, terms = dims
    columns = sources[0].shape[-1]
    block = jax.ShapeDtypeStruct((sec_dev, height, columns), BF16)
    args = [ints, coef, *sources] + ([] if other is None else [other])
    return pl.pallas_call(
        functools.partial(mix_kernel, dims, picks, places, rows_at),
        out_shape=[block] * len(places),
        in_specs=[SMEM, SMEM] + [ANY] * (len(args) - 2),
        out_specs=[VMEM] * len(places),
        scratch_shapes=[
            pltpu.SMEM((sectors,), jnp.int32),
            pltpu.VMEM((2, terms, height, columns), BF16),
            pltpu.SemaphoreType.DMA((2, terms)),
        ],
        compiler_params=pltpu.CompilerParams(vmem_limit_bytes=LIMIT),
        cost_estimate=pl.CostEstimate(
            flops=2 * terms * len(places) * sec_dev * height * columns,
            bytes_accessed=2 * (terms + 1) * len(places) * sec_dev * height * columns,
            transcendentals=0,
        ),
        name="mix",
    )(*args)


def pair_kernel(dims, ops_dev, counts, pieces, first, ints, where, *refs):
    ops, sectors, sec_dev, terms = dims
    grounds, refs = refs[: len(counts)], refs[len(counts) :]
    op_ref, refs = refs[0], refs[1:]
    env_refs, refs = refs[:pieces], refs[pieces:]
    if not first:
        refs = refs[1:]
    out_ref, found, env, ground, result, env_sem, ground_sem, out_sem = refs
    slot_at = ops * sectors
    pos_at = slot_at + sectors + sectors * terms
    me = ints[pos_at]
    op_base = ints[pos_at + 3] * ops_dev
    env_copies = []
    for n in range(pieces):
        start = pl.multiple_of(where[len(counts) + n], 64)
        env_copies.append(
            pltpu.make_async_copy(env_refs[n], env.at[:, pl.ds(start, env_refs[n].shape[1])], env_sem.at[n])
        )
        env_copies[-1].start()

    def search(n, total):
        base = where[n]

        def candidate(s, total):
            for o in range(ops_dev):
                slot = ints[slot_at + ints[(op_base + o) * sectors + base + s]]
                local = slot - me * sec_dev
                mine = jnp.logical_and(local >= 0, local < sec_dev)
                found[0, total] = n
                found[1, total] = s
                found[2, total] = o
                found[3, total] = local
                total = total + mine.astype(jnp.int32)
            return total

        return lax.fori_loop(0, jnp.where(base >= 0, counts[n], 0), candidate, total)

    total = jnp.int32(0)
    for n in range(len(counts)):
        total = search(n, total)

    def fetch(i, side):
        for n in range(len(counts)):

            @pl.when(found[0, i] == n)
            def _(n=n):
                pltpu.make_async_copy(grounds[n].at[found[1, i]], ground.at[side], ground_sem.at[side]).start()

    @pl.when(total > 0)
    def _():
        fetch(0, 0)

    for copy in env_copies:
        copy.wait()

    def step(i, carry):
        side = lax.rem(i, 2)

        @pl.when(i + 1 < total)
        def _():
            fetch(i + 1, 1 - side)

        pltpu.make_async_copy(ground.at[side], ground.at[side], ground_sem.at[side]).wait()
        o, local = found[2, i], found[3, i]
        product = jnp.dot(ground[side], op_ref[o], preferred_element_type=jnp.float32).astype(BF16)
        grown = jnp.dot(product, env[local], preferred_element_type=jnp.float32).astype(BF16)

        @pl.when(i >= 2)
        def _():
            pltpu.make_async_copy(result.at[side], result.at[side], out_sem.at[side]).wait()

        result[side] = grown
        pltpu.make_async_copy(result.at[side], out_ref.at[o, local], out_sem.at[side]).start()
        return carry

    lax.fori_loop(0, total, step, 0)
    for back in (1, 2):

        @pl.when(total >= back)
        def _(back=back):
            side = lax.rem(total - back, 2)
            pltpu.make_async_copy(result.at[side], result.at[side], out_sem.at[side]).wait()


def pairs(dims, ints, where, grounds, op_matrices, env_pieces, out):
    ops, sectors, sec_dev, terms = dims
    ops_dev = op_matrices.shape[0]
    rows, columns = grounds[0].shape[1:]
    counts = [g.shape[0] for g in grounds]
    shape = jax.ShapeDtypeStruct((ops_dev, sec_dev, rows, columns), BF16)
    args = [ints, where, *grounds, op_matrices, *env_pieces] + ([] if out is None else [out])
    work = max(1, sum(counts) * ops_dev * sec_dev // sectors)
    return pl.pallas_call(
        functools.partial(pair_kernel, dims, ops_dev, counts, len(env_pieces), out is None),
        out_shape=shape,
        in_specs=[SMEM, SMEM] + [ANY] * len(grounds) + [VMEM] + [ANY] * (len(args) - 3 - len(grounds)),
        out_specs=ANY,
        scratch_shapes=[
            pltpu.SMEM((4, sum(counts) * ops_dev + 8), jnp.int32),
            pltpu.VMEM((sec_dev, columns, columns), BF16),
            pltpu.VMEM((2, rows, columns), BF16),
            pltpu.VMEM((2, rows, columns), BF16),
            pltpu.SemaphoreType.DMA((len(env_pieces),)),
            pltpu.SemaphoreType.DMA((2,)),
            pltpu.SemaphoreType.DMA((2,)),
        ],
        input_output_aliases={} if out is None else {len(args) - 1: 0},
        compiler_params=pltpu.CompilerParams(vmem_limit_bytes=LIMIT),
        cost_estimate=pl.CostEstimate(
            flops=4 * work * rows * columns * columns,
            bytes_accessed=2 * (2 * work * rows * columns + (ops_dev + sec_dev) * columns * columns),
            transcendentals=0,
        ),
        name="pairs",
    )(*args)


def pack(shift_map, new_slot, env_src, position):
    return jnp.concatenate(
        [shift_map.reshape(-1), new_slot, env_src.reshape(-1), jnp.stack(position).astype(jnp.int32)]
    )


def whole_gather(ground_state, op_matrices, shift_map, new_slot, env_ground, env_src, env_coef):
    owner = lax.axis_index("sec")
    group = lax.axis_index("op")
    halves = lax.axis_size("op")
    sec_dev, rows, columns = ground_state.shape
    ops, sectors = shift_map.shape
    dims = (ops, sectors, sec_dev, env_src.shape[1])
    zero = jnp.zeros((), jnp.int32)
    ints = pack(shift_map, new_slot, env_src, [owner, zero, zero + 1, group])

    def gather(blocks):
        part = rows // halves
        mine = lax.dynamic_slice_in_dim(blocks, group * part, part, 1)
        whole = lax.all_gather(lax.all_gather(mine, "sec", axis=0, tiled=True), "op", axis=1, tiled=True)
        return whole

    env_all = gather(env_ground)
    (env_new,) = mix(dims, ints, env_coef.reshape(-1), [env_all], [None], [0], rows)
    env_rows = lax.all_gather(env_new, "blk", axis=1, tiled=True)
    where = jnp.zeros((2,), jnp.int32)
    return pairs(dims, ints, where, [gather(ground_state)], op_matrices, [env_rows], None)


DEPTH = 4
GROW_COST = 40 * 10**9
MIX_WIDTH = 8
LIST = 16


def device_place():
    owner, core = lax.axis_index("sec"), lax.axis_index("op")
    return owner, core, jnp.where(core == 0, owner, 3 - owner)


def by_spot(spot, values):
    result = jnp.int32(values[0])
    for n in range(1, 4):
        result = jnp.where(spot == n, values[n], result)
    return result


def head_kernel(env, ground, first, second, sems):
    _, _, spot = device_place()
    half = env.shape[1] // 2

    def send(sources):
        copies = [pltpu.make_async_copy(sources[h], (first, second)[h], sems.at[h]) for h in range(2)]
        for copy in copies:
            copy.start()
        for copy in copies:
            copy.wait()

    pl.when(spot == 2)(lambda: send([ground.at[h] for h in range(2)]))
    pl.when(spot != 2)(lambda: send([env.at[:, pl.ds(h * half, half)] for h in range(2)]))


def head(env_ground, ground_half):
    sec_dev, rows, columns = env_ground.shape
    block = jax.ShapeDtypeStruct((sec_dev, rows // 2, columns), BF16)
    return pl.pallas_call(
        head_kernel,
        out_shape=[block, block],
        in_specs=[HBM, HBM],
        out_specs=[VMEM, VMEM],
        scratch_shapes=[pltpu.SemaphoreType.DMA((2,))],
        compiler_params=pltpu.CompilerParams(vmem_limit_bytes=LARGE),
        cost_estimate=pl.CostEstimate(flops=0, bytes_accessed=4 * sec_dev * rows * columns, transcendentals=0),
        name="head",
    )(env_ground, ground_half)


def tables_kernel(dims, ops_dev, shift, slot, src, table, inverse):
    ops, sectors, sec_dev, terms = dims
    owner, core, _ = device_place()
    ahead = jnp.where(core == 0, jnp.minimum(owner + 1, 3), jnp.maximum(owner - 1, 0))

    def invert(t, carry):
        inverse[slot[t]] = t
        return carry

    lax.fori_loop(0, sectors, invert, 0)

    def terms_of(i, carry):
        place = jnp.where(i < sec_dev, ahead * sec_dev + i, owner * sec_dev + i - sec_dev)
        t = inverse[place]
        table[i * MIX_WIDTH] = t
        for k in range(terms):
            source = src[k, t]
            from_owner = source // sec_dev
            table[i * MIX_WIDTH + 1 + 2 * k] = jnp.where(core == 0, from_owner, 3 - from_owner)
            table[i * MIX_WIDTH + 2 + 2 * k] = source - from_owner * sec_dev
        return carry

    lax.fori_loop(0, 2 * sec_dev, terms_of, 0)
    count_at = 2 * sec_dev * MIX_WIDTH
    list_at = count_at + 8
    width = sec_dev // 2

    def pairs_of(n, carry):
        total = jnp.int32(0)
        for s in range(width):
            for o in range(ops_dev):
                local = slot[shift[core * ops_dev + o, n * width + s]] - owner * sec_dev
                table[list_at + n * LIST + total] = (s * ops_dev + o) * sec_dev + local
                total = total + jnp.logical_and(local >= 0, local < sec_dev).astype(jnp.int32)
        table[count_at + n] = total
        return carry

    lax.fori_loop(0, sectors // width, pairs_of, 0)


def tables(dims, ops_dev, shift_map, new_slot, env_src):
    ops, sectors, sec_dev, terms = dims
    return pl.pallas_call(
        functools.partial(tables_kernel, dims, ops_dev),
        out_shape=jax.ShapeDtypeStruct((2 * sec_dev * MIX_WIDTH + 8 + 8 * LIST,), jnp.int32),
        in_specs=[SMEM, SMEM, SMEM],
        out_specs=SMEM,
        scratch_shapes=[pltpu.SMEM((sectors,), jnp.int32)],
        cost_estimate=pl.CostEstimate(flops=10000, bytes_accessed=4000, transcendentals=0),
        name="tables",
    )(shift_map, new_slot, env_src)


def blend_kernel(dims, which, table, coef, second, first, env, other, ground, passed, made, held, sems):
    ops, sectors, sec_dev, terms = dims
    _, _, spot = device_place()
    height = held.shape[2]
    sources = [second, first, env.at[:, pl.ds(which * height, height)], other]

    @pl.when(spot == 2)
    def _():
        def fetch(i, carry):
            for k in range(terms):
                code, block = table[i * MIX_WIDTH + 1 + 2 * k], table[i * MIX_WIDTH + 2 + 2 * k]
                for q in range(4):

                    @pl.when(code == q)
                    def _(q=q, k=k, block=block):
                        pltpu.make_async_copy(sources[q].at[block], held.at[i, k], sems.at[i]).start()

            return carry

        lax.fori_loop(0, 2 * sec_dev, fetch, 0)

        def sums(out, lead):
            def one(i, carry):
                at = i + lead
                pltpu.make_async_copy(held.at[at], held.at[at], sems.at[at]).wait()
                t = table[at * MIX_WIDTH]
                weights = [coef[k, t] for k in range(terms)]
                for r in range(0, height, 32):
                    total = weights[0] * held[at, 0, r : r + 32].astype(jnp.float32)
                    for k in range(1, terms):
                        total += weights[k] * held[at, k, r : r + 32].astype(jnp.float32)
                    out[i, r : r + 32] = total.astype(BF16)
                return carry

            lax.fori_loop(0, sec_dev, one, 0)

        sums(passed, 0)
        sums(made, sec_dev)

    @pl.when(spot != 2)
    def _():
        copy = pltpu.make_async_copy(ground.at[which], passed, sems.at[0])
        copy.start()
        copy.wait()


def blend(dims, which, table, coef, second, first, env_ground, other, ground_half):
    ops, sectors, sec_dev, terms = dims
    block = jax.ShapeDtypeStruct(first.shape, BF16)
    _, height, columns = first.shape
    return pl.pallas_call(
        functools.partial(blend_kernel, dims, which),
        out_shape=[block, block],
        in_specs=[SMEM, SMEM] + [HBM] * 5,
        out_specs=[VMEM, VMEM],
        scratch_shapes=[
            pltpu.VMEM((2 * sec_dev, terms, height, columns), BF16),
            pltpu.SemaphoreType.DMA((2 * sec_dev,)),
        ],
        compiler_params=pltpu.CompilerParams(vmem_limit_bytes=MEDIUM),
        cost_estimate=pl.CostEstimate(
            flops=4 * terms * sec_dev * height * columns,
            bytes_accessed=4 * (terms + 1) * sec_dev * height * columns,
            transcendentals=0,
        ),
        name="blend",
    )(table, coef, second, first, env_ground, other, ground_half)


def half_owner(owner, core, spot, hops, h, sibling):
    if hops is None:
        return 2 * owner + h
    n = by_spot(3 - spot if sibling else spot, hops)
    back = jnp.where(core == 0, -1, 1) * (-1 if sibling else 1)
    return jnp.where(n > 0, 2 * (owner + back * n) + h, -1)


def grow_kernel(dims, ops_dev, parts, arrays, table, *refs):
    ops, sectors, sec_dev, terms = dims
    grounds, op_ref, refs = refs[:arrays], refs[arrays], refs[arrays + 1 :]
    owner, core, spot = device_place()
    rows, columns = grounds[0].shape[1:]
    width = sec_dev // 2
    pieces, (out_ref, env, found, ground, result, ground_sem, out_sem, env_sem) = refs[:4], refs[4:]
    count_at = 2 * sec_dev * MIX_WIDTH
    list_at = count_at + 8
    part_of = [half_owner(owner, core, spot, hops, h, sibling) for _, hops, h, sibling, _ in parts]
    for m, (n, _, _, _, lead) in enumerate(parts):

        @pl.when(part_of[m] >= 0)
        def _(m=m, n=n, lead=lead):
            source = grounds[n].at[pl.ds(lead, width)]
            pltpu.make_async_copy(source, ground.at[pl.ds(m * width, width)], ground_sem.at[m]).start()

    env_copies = []
    half = rows // 2
    own = lax.axis_index("blk") * rows
    lead = spot >= 2
    starts = [jnp.where(lead, own, rows - own), jnp.where(lead, rows - own, own)]
    for n in range(4):
        start = pl.multiple_of(starts[n % 2] + n // 2 * half, half)
        env_copies.append(pltpu.make_async_copy(pieces[n], env.at[:, pl.ds(start, half)], env_sem.at[n]))
        env_copies[-1].start()

    total = jnp.int32(0)
    for m in range(len(parts)):
        part = part_of[m]
        count = jnp.where(part >= 0, table[count_at + jnp.maximum(part, 0)], 0)

        def take(i, carry, total=total, part=part, m=m):
            entry = table[list_at + part * LIST + i]
            rest = entry // sec_dev
            found[0, total + i] = m * width + rest // ops_dev
            found[1, total + i] = lax.rem(rest, ops_dev)
            found[2, total + i] = lax.rem(entry, sec_dev)
            return carry

        lax.fori_loop(0, count, take, 0)
        total = total + count
    for copy in env_copies:
        copy.wait()
    for m in range(len(parts)):

        @pl.when(part_of[m] >= 0)
        def _(m=m):
            here = ground.at[pl.ds(m * width, width)]
            pltpu.make_async_copy(here, here, ground_sem.at[m]).wait()

    def drain(side):
        pltpu.make_async_copy(result.at[side], result.at[side], out_sem.at[side]).wait()

    def step(i, carry):
        side = lax.rem(i, DEPTH)
        o, local = found[1, i], found[2, i]
        product = jnp.dot(ground[found[0, i]], op_ref[o], preferred_element_type=jnp.float32).astype(BF16)
        grown = jnp.dot(product, env[local], preferred_element_type=jnp.float32).astype(BF16)
        pl.when(i >= DEPTH)(lambda: drain(side))
        result[side] = grown
        pltpu.make_async_copy(result.at[side], out_ref.at[o, local], out_sem.at[side]).start()
        return carry

    lax.fori_loop(0, total, step, 0)
    for back in range(1, DEPTH + 1):
        pl.when(total >= back)(lambda back=back: drain(lax.rem(total - back, DEPTH)))


def grow(dims, table, parts, grounds, op_matrices, pieces):
    ops, sectors, sec_dev, terms = dims
    ops_dev = op_matrices.shape[0]
    rows, columns = grounds[0].shape[1:]
    return pl.pallas_call(
        functools.partial(grow_kernel, dims, ops_dev, parts, len(grounds)),
        out_shape=[
            jax.ShapeDtypeStruct((ops_dev, sec_dev, rows, columns), BF16),
            jax.ShapeDtypeStruct((sec_dev, columns, columns), BF16),
        ],
        in_specs=[SMEM] + [ANY] * len(grounds) + [VMEM] + [ANY] * len(pieces),
        out_specs=[ANY, VMEM],
        scratch_shapes=[
            pltpu.SMEM((3, LIST * len(parts)), jnp.int32),
            pltpu.VMEM((sec_dev // 2 * len(parts), rows, columns), BF16),
            pltpu.VMEM((DEPTH, rows, columns), BF16),
            pltpu.SemaphoreType.DMA((len(parts),)),
            pltpu.SemaphoreType.DMA((DEPTH,)),
            pltpu.SemaphoreType.DMA((4,)),
        ],
        compiler_params=pltpu.CompilerParams(vmem_limit_bytes=MEDIUM),
        cost_estimate=pl.CostEstimate(flops=1 << 20, bytes_accessed=1 << 12, transcendentals=0),
        name="grow",
    )(table, *grounds, op_matrices, *pieces)


def finish_kernel(dims, ops_dev, table, own_a, other_a, own_b, other_b, op_ref, env, _, out_ref, found, result, out_sem):
    ops, sectors, sec_dev, terms = dims
    owner, core, spot = device_place()
    count_at = 2 * sec_dev * MIX_WIDTH
    list_at = count_at + 8
    total = jnp.int32(0)
    for h in range(2):
        part = jnp.where(spot == 3, half_owner(owner, core, spot, [0, 0, 0, 3], h, False), -1)
        part = jnp.where(spot == 0, half_owner(owner, core, spot, [0, 0, 0, 3], h, True), part)
        count = jnp.where(part >= 0, table[count_at + jnp.maximum(part, 0)], 0)

        def take(n, carry, part=part, total=total, h=h):
            entry = table[list_at + part * LIST + n]
            rest = entry // sec_dev
            found[0, total + n] = h
            found[1, total + n] = rest // ops_dev
            found[2, total + n] = lax.rem(rest, ops_dev)
            found[3, total + n] = lax.rem(entry, sec_dev)
            return carry

        lax.fori_loop(0, count, take, 0)
        total = total + count

    def drain(side):
        pltpu.make_async_copy(result.at[side], result.at[side], out_sem.at[side]).wait()

    def step(i, carry):
        side = lax.rem(i, DEPTH)
        h, s, o, local = (found[k, i] for k in range(4))
        first = jnp.where(spot == 3, own_a[s], other_a[s])
        second = jnp.where(spot == 3, own_b[s], other_b[s])
        block = jnp.where(h == 0, first, second)
        product = jnp.dot(block, op_ref[o], preferred_element_type=jnp.float32).astype(BF16)
        grown = jnp.dot(product, env[local], preferred_element_type=jnp.float32).astype(BF16)
        pl.when(i >= DEPTH)(lambda: drain(side))
        result[side] = grown
        pltpu.make_async_copy(result.at[side], out_ref.at[o, local], out_sem.at[side]).start()
        return carry

    lax.fori_loop(0, total, step, 0)
    for back in range(1, DEPTH + 1):
        pl.when(total >= back)(lambda back=back: drain(lax.rem(total - back, DEPTH)))


def finish(dims, table, ends, op_matrices, env, out):
    ops, sectors, sec_dev, terms = dims
    ops_dev, _, rows, columns = out.shape
    return pl.pallas_call(
        functools.partial(finish_kernel, dims, ops_dev),
        out_shape=jax.ShapeDtypeStruct(out.shape, BF16),
        in_specs=[SMEM] + [VMEM] * 6 + [ANY],
        out_specs=ANY,
        scratch_shapes=[
            pltpu.SMEM((4, sec_dev * ops_dev), jnp.int32),
            pltpu.VMEM((DEPTH, rows, columns), BF16),
            pltpu.SemaphoreType.DMA((DEPTH,)),
        ],
        input_output_aliases={7: 0},
        compiler_params=pltpu.CompilerParams(vmem_limit_bytes=MEDIUM),
        cost_estimate=pl.CostEstimate(flops=GROW_COST, bytes_accessed=1 << 20, transcendentals=0),
        name="finish",
    )(table, *ends, op_matrices, env, out)


def line_of_four(ground_state, op_matrices, shift_map, new_slot, env_ground, env_src, env_coef):
    _, _, spot = device_place()
    sec_dev, rows, columns = ground_state.shape
    ops, sectors = shift_map.shape
    ops_dev = op_matrices.shape[0]
    dims = (ops, sectors, sec_dev, env_src.shape[1])
    half = rows // 2

    def stream(steps):
        up = [(2 * a, 2 * a + 2) for a in steps]
        down = [(2 * (3 - a) + 1, 2 * (2 - a) + 1) for a in steps]
        return lambda block: lax.ppermute(block, ("sec", "op"), up + down)

    def hand(block, spots):
        pairs_of = [(2 * z + core, 2 * z + 1 - core) for spot in spots for z, core in at[spot]]
        return lax.ppermute(block, ("sec", "op"), pairs_of)

    def across(block):
        leads = at[2] + at[3]
        pairs_of = [((z * 2 + x) * 2 + core, (z * 2 + 1 - x) * 2 + 1 - core) for z, core in leads for x in range(2)]
        return lax.ppermute(block, ("sec", "blk", "op"), pairs_of)

    def after(block, *others):
        return lax.optimization_barrier((block, *others))[0]

    at = [[(0, 0), (3, 1)], [(1, 0), (2, 1)], [(2, 0), (1, 1)], [(3, 0), (0, 1)]]
    every, middle, late, last = stream([0, 1, 2]), stream([1]), stream([1, 2]), stream([2])
    ground_half = ground_state.reshape(2, sec_dev, half, columns)
    both = range(2)

    sent0 = head(env_ground, ground_half)
    got0 = [every(sent0[h]) for h in both]
    got2 = [middle(got0[h]) for h in both]
    swapped0 = [hand(got0[h], [1, 3]) for h in both]
    table = tables(dims, ops_dev, shift_map, new_slot, env_src.T)
    sent4, made = zip(
        *[blend(dims, h, table, env_coef.T, got2[h], got0[h], env_ground, swapped0[h], ground_half) for h in both]
    )
    got4 = [every(sent4[h]) for h in both]
    got6 = [late(got4[h]) for h in both]
    swapped4 = [hand(got4[h], [1, 2, 3]) for h in both]
    swapped6 = [hand(got6[h], [2, 3]) for h in both]
    pieces = []
    for h in both:
        mine = jnp.where(spot == 2, made[h], got4[h])
        received = after(across(mine), got6[h])
        kept = jnp.where(spot >= 2, mine, received)
        pieces += [kept, hand(kept, [0, 1, 2, 3])]
    got8 = [last(got6[0]), last(after(got6[1], *swapped4, swapped6[0], pieces[1]))]

    parts = [(0, None, h, False, h * sec_dev // 2) for h in both]
    arrays = [ground_state]

    def hold(mine, theirs, hops, h):
        for block, sibling in ((mine, False), (theirs, True)):
            parts.append((len(arrays), hops, h, sibling, 0))
            arrays.append(block.reshape(sec_dev // 2, rows, columns))

    for h in both:
        hold(got0[h], swapped0[h], [0, 0, 0, 1], h)
        hold(got4[h], swapped4[h], [0, 1, 1, 0], h)
    for h in both:
        hold(got6[h], swapped6[h], [0, 0, 2, 2], h)
    out, env = grow(dims, table, parts, arrays, op_matrices, pieces)
    swapped8 = [hand(after(got8[h], out), [3]) for h in both]
    ends = [block[h].reshape(sec_dev // 2, rows, columns) for h in both for block in (got8, swapped8)]
    return finish(dims, table, ends, op_matrices, env, out)


def solution(mesh):
    four = mesh.shape["sec"] == 4 and mesh.shape["blk"] == 2 and mesh.shape["op"] == 2
    return jax.shard_map(
        line_of_four if four else whole_gather,
        mesh=mesh,
        in_specs=(
            P(("grp", "sec"), "blk", None),
            P(("grp", "op"), None, None),
            P("grp", None),
            P("grp"),
            P(("grp", "sec"), "blk", None),
            P("grp", None),
            P("grp", None),
        ),
        out_specs=P(("grp", "op"), "sec", "blk", None),
        check_vma=False,
    )
```

```python
import functools

import jax
import jax.numpy as jnp
from jax import lax
from jax.experimental import pallas as pl
from jax.experimental.pallas import tpu as pltpu
from jax.sharding import PartitionSpec as P

ANY = pl.BlockSpec(memory_space=pl.ANY)
HBM = pl.BlockSpec(memory_space=pltpu.HBM)
SMEM = pl.BlockSpec(memory_space=pltpu.SMEM)
VMEM = pl.BlockSpec(memory_space=pltpu.VMEM)
BF16 = jnp.bfloat16
LIMIT = 40 << 20
LARGE = 60 << 20
MEDIUM = 28 << 20


def mix_kernel(dims, picks, places, rows_at, ints, coef, *refs):
    ops, sectors, sec_dev, terms = dims
    count = len(picks)
    sources, refs = refs[:count], refs[count:]
    other = None
    if rows_at is not None:
        other, refs = refs[0], refs[1:]
    outs, (inverse, held, sems) = refs[: len(places)], refs[len(places) :]
    slot_at = ops * sectors
    src_at = slot_at + sectors
    pos_at = src_at + sectors * terms
    busy = ints[pos_at + 2] == 1

    def compute():
        def invert(t, carry):
            inverse[ints[slot_at + t]] = t
            return carry

        lax.fori_loop(0, sectors, invert, 0)

        def copies(place, i, side, act):
            owner = ints[pos_at + place]
            t = inverse[owner * sec_dev + i]
            for k in range(terms):
                source = ints[src_at + t * terms + k]
                if count == 1:
                    act(pltpu.make_async_copy(sources[0].at[source], held.at[side, k], sems.at[side, k]))
                    continue
                code = ints[pos_at + 16 + source // sec_dev]
                for q in range(count):

                    @pl.when(code == q)
                    def _(q=q, k=k, source=source):
                        src = sources[q].at[source % sec_dev]
                        if picks[q] is not None:
                            src = src.at[pl.ds(picks[q], held.shape[2])]
                        act(pltpu.make_async_copy(src, held.at[side, k], sems.at[side, k]))

        steps = [(n, place) for n, place in enumerate(places)]
        for n, place in steps:
            copies(place, 0, 0, lambda c: c.start())

            def step(i, carry, n=n, place=place):
                side = lax.rem(i, 2)

                @pl.when(i + 1 < sec_dev)
                def _():
                    copies(place, i + 1, 1 - side, lambda c: c.start())

                for k in range(terms):
                    pltpu.make_async_copy(held.at[side, k], held.at[side, k], sems.at[side, k]).wait()
                t = inverse[ints[pos_at + place] * sec_dev + i]
                height = min(32, held.shape[2])
                for r in range(0, held.shape[2], height):
                    total = coef[t * terms] * held[side, 0, r : r + height].astype(jnp.float32)
                    for k in range(1, terms):
                        total += coef[t * terms + k] * held[side, k, r : r + height].astype(jnp.float32)
                    outs[n][i, r : r + height] = total.astype(BF16)
                return carry

            lax.fori_loop(0, sec_dev, step, 0)

    if other is None:
        compute()
        return
    pl.when(busy)(compute)

    @pl.when(jnp.logical_not(busy))
    def _():
        copy = pltpu.make_async_copy(other.at[rows_at], outs[0], sems.at[0, 0])
        copy.start()
        copy.wait()


def mix(dims, ints, coef, sources, picks, places, height, other=None, rows_at=None):
    ops, sectors, sec_dev, terms = dims
    columns = sources[0].shape[-1]
    block = jax.ShapeDtypeStruct((sec_dev, height, columns), BF16)
    args = [ints, coef, *sources] + ([] if other is None else [other])
    return pl.pallas_call(
        functools.partial(mix_kernel, dims, picks, places, rows_at),
        out_shape=[block] * len(places),
        in_specs=[SMEM, SMEM] + [ANY] * (len(args) - 2),
        out_specs=[VMEM] * len(places),
        scratch_shapes=[
            pltpu.SMEM((sectors,), jnp.int32),
            pltpu.VMEM((2, terms, height, columns), BF16),
            pltpu.SemaphoreType.DMA((2, terms)),
        ],
        compiler_params=pltpu.CompilerParams(vmem_limit_bytes=LIMIT),
        cost_estimate=pl.CostEstimate(
            flops=2 * terms * len(places) * sec_dev * height * columns,
            bytes_accessed=2 * (terms + 1) * len(places) * sec_dev * height * columns,
            transcendentals=0,
        ),
        name="mix",
    )(*args)


def pair_kernel(dims, ops_dev, counts, pieces, first, ints, where, *refs):
    ops, sectors, sec_dev, terms = dims
    grounds, refs = refs[: len(counts)], refs[len(counts) :]
    op_ref, refs = refs[0], refs[1:]
    env_refs, refs = refs[:pieces], refs[pieces:]
    if not first:
        refs = refs[1:]
    out_ref, found, env, ground, result, env_sem, ground_sem, out_sem = refs
    slot_at = ops * sectors
    pos_at = slot_at + sectors + sectors * terms
    me = ints[pos_at]
    op_base = ints[pos_at + 3] * ops_dev
    env_copies = []
    for n in range(pieces):
        start = pl.multiple_of(where[len(counts) + n], 64)
        env_copies.append(
            pltpu.make_async_copy(env_refs[n], env.at[:, pl.ds(start, env_refs[n].shape[1])], env_sem.at[n])
        )
        env_copies[-1].start()

    def search(n, total):
        base = where[n]

        def candidate(s, total):
            for o in range(ops_dev):
                slot = ints[slot_at + ints[(op_base + o) * sectors + base + s]]
                local = slot - me * sec_dev
                mine = jnp.logical_and(local >= 0, local < sec_dev)
                found[0, total] = n
                found[1, total] = s
                found[2, total] = o
                found[3, total] = local
                total = total + mine.astype(jnp.int32)
            return total

        return lax.fori_loop(0, jnp.where(base >= 0, counts[n], 0), candidate, total)

    total = jnp.int32(0)
    for n in range(len(counts)):
        total = search(n, total)

    def fetch(i, side):
        for n in range(len(counts)):

            @pl.when(found[0, i] == n)
            def _(n=n):
                pltpu.make_async_copy(grounds[n].at[found[1, i]], ground.at[side], ground_sem.at[side]).start()

    @pl.when(total > 0)
    def _():
        fetch(0, 0)

    for copy in env_copies:
        copy.wait()

    def step(i, carry):
        side = lax.rem(i, 2)

        @pl.when(i + 1 < total)
        def _():
            fetch(i + 1, 1 - side)

        pltpu.make_async_copy(ground.at[side], ground.at[side], ground_sem.at[side]).wait()
        o, local = found[2, i], found[3, i]
        product = jnp.dot(ground[side], op_ref[o], preferred_element_type=jnp.float32).astype(BF16)
        grown = jnp.dot(product, env[local], preferred_element_type=jnp.float32).astype(BF16)

        @pl.when(i >= 2)
        def _():
            pltpu.make_async_copy(result.at[side], result.at[side], out_sem.at[side]).wait()

        result[side] = grown
        pltpu.make_async_copy(result.at[side], out_ref.at[o, local], out_sem.at[side]).start()
        return carry

    lax.fori_loop(0, total, step, 0)
    for back in (1, 2):

        @pl.when(total >= back)
        def _(back=back):
            side = lax.rem(total - back, 2)
            pltpu.make_async_copy(result.at[side], result.at[side], out_sem.at[side]).wait()


def pairs(dims, ints, where, grounds, op_matrices, env_pieces, out):
    ops, sectors, sec_dev, terms = dims
    ops_dev = op_matrices.shape[0]
    rows, columns = grounds[0].shape[1:]
    counts = [g.shape[0] for g in grounds]
    shape = jax.ShapeDtypeStruct((ops_dev, sec_dev, rows, columns), BF16)
    args = [ints, where, *grounds, op_matrices, *env_pieces] + ([] if out is None else [out])
    work = max(1, sum(counts) * ops_dev * sec_dev // sectors)
    return pl.pallas_call(
        functools.partial(pair_kernel, dims, ops_dev, counts, len(env_pieces), out is None),
        out_shape=shape,
        in_specs=[SMEM, SMEM] + [ANY] * len(grounds) + [VMEM] + [ANY] * (len(args) - 3 - len(grounds)),
        out_specs=ANY,
        scratch_shapes=[
            pltpu.SMEM((4, sum(counts) * ops_dev + 8), jnp.int32),
            pltpu.VMEM((sec_dev, columns, columns), BF16),
            pltpu.VMEM((2, rows, columns), BF16),
            pltpu.VMEM((2, rows, columns), BF16),
            pltpu.SemaphoreType.DMA((len(env_pieces),)),
            pltpu.SemaphoreType.DMA((2,)),
            pltpu.SemaphoreType.DMA((2,)),
        ],
        input_output_aliases={} if out is None else {len(args) - 1: 0},
        compiler_params=pltpu.CompilerParams(vmem_limit_bytes=LIMIT),
        cost_estimate=pl.CostEstimate(
            flops=4 * work * rows * columns * columns,
            bytes_accessed=2 * (2 * work * rows * columns + (ops_dev + sec_dev) * columns * columns),
            transcendentals=0,
        ),
        name="pairs",
    )(*args)


def pack(shift_map, new_slot, env_src, position):
    return jnp.concatenate(
        [shift_map.reshape(-1), new_slot, env_src.reshape(-1), jnp.stack(position).astype(jnp.int32)]
    )


def whole_gather(ground_state, op_matrices, shift_map, new_slot, env_ground, env_src, env_coef):
    owner = lax.axis_index("sec")
    group = lax.axis_index("op")
    halves = lax.axis_size("op")
    sec_dev, rows, columns = ground_state.shape
    ops, sectors = shift_map.shape
    dims = (ops, sectors, sec_dev, env_src.shape[1])
    zero = jnp.zeros((), jnp.int32)
    ints = pack(shift_map, new_slot, env_src, [owner, zero, zero + 1, group])

    def gather(blocks):
        part = rows // halves
        mine = lax.dynamic_slice_in_dim(blocks, group * part, part, 1)
        whole = lax.all_gather(lax.all_gather(mine, "sec", axis=0, tiled=True), "op", axis=1, tiled=True)
        return whole

    env_all = gather(env_ground)
    (env_new,) = mix(dims, ints, env_coef.reshape(-1), [env_all], [None], [0], rows)
    env_rows = lax.all_gather(env_new, "blk", axis=1, tiled=True)
    where = jnp.zeros((2,), jnp.int32)
    return pairs(dims, ints, where, [gather(ground_state)], op_matrices, [env_rows], None)


DEPTH = 4
MIX_WIDTH = 8
LIST = 16


def device_place():
    owner, core = lax.axis_index("sec"), lax.axis_index("op")
    return owner, core, jnp.where(core == 0, owner, 3 - owner)


def by_spot(spot, values):
    result = jnp.int32(values[0])
    for n in range(1, 4):
        result = jnp.where(spot == n, values[n], result)
    return result


def head_kernel(h, env, ground, sent, sem):
    _, _, spot = device_place()
    half = env.shape[1] // 2

    def send(source):
        copy = pltpu.make_async_copy(source, sent, sem)
        copy.start()
        copy.wait()

    pl.when(spot == 2)(lambda: send(ground.at[h]))
    pl.when(spot != 2)(lambda: send(env.at[:, pl.ds(h * half, half)]))


def head(h, env_ground, ground_half):
    sec_dev, rows, columns = env_ground.shape
    return pl.pallas_call(
        functools.partial(head_kernel, h),
        out_shape=jax.ShapeDtypeStruct((sec_dev, rows // 2, columns), BF16),
        in_specs=[HBM, HBM],
        out_specs=VMEM,
        scratch_shapes=[pltpu.SemaphoreType.DMA],
        compiler_params=pltpu.CompilerParams(vmem_limit_bytes=LARGE),
        cost_estimate=pl.CostEstimate(flops=0, bytes_accessed=2 * sec_dev * rows * columns, transcendentals=0),
        name="head",
    )(env_ground, ground_half)


def tables_kernel(dims, ops_dev, shift, slot, src, table, inverse):
    ops, sectors, sec_dev, terms = dims
    owner, core, _ = device_place()
    ahead = jnp.where(core == 0, jnp.minimum(owner + 1, 3), jnp.maximum(owner - 1, 0))

    def invert(t, carry):
        inverse[slot[t]] = t
        return carry

    lax.fori_loop(0, sectors, invert, 0)

    def terms_of(i, carry):
        place = jnp.where(i < sec_dev, ahead * sec_dev + i, owner * sec_dev + i - sec_dev)
        t = inverse[place]
        table[i * MIX_WIDTH] = t
        for k in range(terms):
            source = src[k, t]
            from_owner = source // sec_dev
            table[i * MIX_WIDTH + 1 + 2 * k] = jnp.where(core == 0, from_owner, 3 - from_owner)
            table[i * MIX_WIDTH + 2 + 2 * k] = source - from_owner * sec_dev
        return carry

    lax.fori_loop(0, 2 * sec_dev, terms_of, 0)
    count_at = 2 * sec_dev * MIX_WIDTH
    list_at = count_at + 8
    width = sec_dev // 2

    def pairs_of(n, carry):
        total = jnp.int32(0)
        for s in range(width):
            for o in range(ops_dev):
                local = slot[shift[core * ops_dev + o, n * width + s]] - owner * sec_dev
                table[list_at + n * LIST + total] = (s * ops_dev + o) * sec_dev + local
                total = total + jnp.logical_and(local >= 0, local < sec_dev).astype(jnp.int32)
        table[count_at + n] = total
        return carry

    lax.fori_loop(0, sectors // width, pairs_of, 0)


def tables(dims, ops_dev, shift_map, new_slot, env_src):
    ops, sectors, sec_dev, terms = dims
    return pl.pallas_call(
        functools.partial(tables_kernel, dims, ops_dev),
        out_shape=jax.ShapeDtypeStruct((2 * sec_dev * MIX_WIDTH + 8 + 8 * LIST,), jnp.int32),
        in_specs=[SMEM, SMEM, SMEM],
        out_specs=SMEM,
        scratch_shapes=[pltpu.SMEM((sectors,), jnp.int32)],
        cost_estimate=pl.CostEstimate(flops=10000, bytes_accessed=4000, transcendentals=0),
        name="tables",
    )(shift_map, new_slot, env_src)


def blend_kernel(dims, which, table, coef, second, first, env, other, ground, passed, made, held, sems):
    ops, sectors, sec_dev, terms = dims
    _, _, spot = device_place()
    height = held.shape[2]
    sources = [second, first, env.at[:, pl.ds(which * height, height)], other]

    @pl.when(spot == 2)
    def _():
        def fetch(i, carry):
            for k in range(terms):
                code, block = table[i * MIX_WIDTH + 1 + 2 * k], table[i * MIX_WIDTH + 2 + 2 * k]
                for q in range(4):

                    @pl.when(code == q)
                    def _(q=q, k=k, block=block):
                        pltpu.make_async_copy(sources[q].at[block], held.at[i, k], sems.at[i]).start()

            return carry

        lax.fori_loop(0, 2 * sec_dev, fetch, 0)

        def sums(out, lead):
            def one(i, carry):
                at = i + lead
                pltpu.make_async_copy(held.at[at], held.at[at], sems.at[at]).wait()
                t = table[at * MIX_WIDTH]
                weights = [coef[k, t] for k in range(terms)]
                for r in range(0, height, 32):
                    total = weights[0] * held[at, 0, r : r + 32].astype(jnp.float32)
                    for k in range(1, terms):
                        total += weights[k] * held[at, k, r : r + 32].astype(jnp.float32)
                    out[i, r : r + 32] = total.astype(BF16)
                return carry

            lax.fori_loop(0, sec_dev, one, 0)

        sums(passed, 0)
        sums(made, sec_dev)

    @pl.when(spot != 2)
    def _():
        copy = pltpu.make_async_copy(ground.at[which], passed, sems.at[0])
        copy.start()
        copy.wait()


def blend(dims, which, table, coef, second, first, env_ground, other, ground_half):
    ops, sectors, sec_dev, terms = dims
    block = jax.ShapeDtypeStruct(first.shape, BF16)
    _, height, columns = first.shape
    return pl.pallas_call(
        functools.partial(blend_kernel, dims, which),
        out_shape=[block, block],
        in_specs=[SMEM, SMEM] + [HBM] * 5,
        out_specs=[VMEM, VMEM],
        scratch_shapes=[
            pltpu.VMEM((2 * sec_dev, terms, height, columns), BF16),
            pltpu.SemaphoreType.DMA((2 * sec_dev,)),
        ],
        compiler_params=pltpu.CompilerParams(vmem_limit_bytes=MEDIUM),
        cost_estimate=pl.CostEstimate(
            flops=4 * terms * sec_dev * height * columns,
            bytes_accessed=4 * (terms + 1) * sec_dev * height * columns,
            transcendentals=0,
        ),
        name="blend",
    )(table, coef, second, first, env_ground, other, ground_half)


def half_owner(owner, core, spot, hops, h, sibling):
    if hops is None:
        return 2 * owner + h
    n = by_spot(3 - spot if sibling else spot, hops)
    back = jnp.where(core == 0, -1, 1) * (-1 if sibling else 1)
    return jnp.where(n > 0, 2 * (owner + back * n) + h, -1)


def grow_kernel(dims, ops_dev, parts, arrays, table, *refs):
    ops, sectors, sec_dev, terms = dims
    grounds, op_ref, refs = refs[:arrays], refs[arrays], refs[arrays + 1 :]
    owner, core, spot = device_place()
    rows, columns = grounds[0].shape[1:]
    width = sec_dev // 2
    pieces, (out_ref, env, found, ground, result, ground_sem, out_sem, env_sem) = refs[:12], refs[12:]
    count_at = 2 * sec_dev * MIX_WIDTH
    list_at = count_at + 8
    part_of = [half_owner(owner, core, spot, hops, h, sibling) for _, hops, h, sibling, _ in parts]
    for m, (n, _, _, _, lead) in enumerate(parts):

        @pl.when(part_of[m] >= 0)
        def _(m=m, n=n, lead=lead):
            source = grounds[n].at[pl.ds(lead, width)]
            pltpu.make_async_copy(source, ground.at[pl.ds(m * width, width)], ground_sem.at[m]).start()

    env_copies = []
    half = rows // 2
    own = lax.axis_index("blk") * rows
    for h in range(2):
        made, near, got, swapped, far, back = pieces[6 * h : 6 * h + 6]
        choices = [[swapped, near, made, got], [far, far, back, back]]
        for n, start in enumerate((own + h * half, rows - own + h * half)):
            target = env.at[:, pl.ds(pl.multiple_of(start, half), half)]
            for q in range(4):

                @pl.when(spot == q)
                def _(source=choices[n][q], target=target, sem=env_sem.at[2 * h + n]):
                    pltpu.make_async_copy(source, target, sem).start()

            env_copies.append(pltpu.make_async_copy(target, target, env_sem.at[2 * h + n]))

    total = jnp.int32(0)
    for m in range(len(parts)):
        part = part_of[m]
        count = jnp.where(part >= 0, table[count_at + jnp.maximum(part, 0)], 0)

        def take(i, carry, total=total, part=part, m=m):
            entry = table[list_at + part * LIST + i]
            rest = entry // sec_dev
            found[0, total + i] = m * width + rest // ops_dev
            found[1, total + i] = lax.rem(rest, ops_dev)
            found[2, total + i] = lax.rem(entry, sec_dev)
            return carry

        lax.fori_loop(0, count, take, 0)
        total = total + count
    for copy in env_copies:
        copy.wait()
    for m in range(len(parts)):

        @pl.when(part_of[m] >= 0)
        def _(m=m):
            here = ground.at[pl.ds(m * width, width)]
            pltpu.make_async_copy(here, here, ground_sem.at[m]).wait()

    def drain(side):
        pltpu.make_async_copy(result.at[side], result.at[side], out_sem.at[side]).wait()

    def step(i, carry):
        side = lax.rem(i, DEPTH)
        o, local = found[1, i], found[2, i]
        product = jnp.dot(ground[found[0, i]], op_ref[o], preferred_element_type=jnp.float32).astype(BF16)
        grown = jnp.dot(product, env[local], preferred_element_type=jnp.float32).astype(BF16)
        pl.when(i >= DEPTH)(lambda: drain(side))
        result[side] = grown
        pltpu.make_async_copy(result.at[side], out_ref.at[o, local], out_sem.at[side]).start()
        return carry

    lax.fori_loop(0, total, step, 0)
    for back in range(1, DEPTH + 1):
        pl.when(total >= back)(lambda back=back: drain(lax.rem(total - back, DEPTH)))


def grow(dims, table, parts, grounds, op_matrices, pieces):
    ops, sectors, sec_dev, terms = dims
    ops_dev = op_matrices.shape[0]
    rows, columns = grounds[0].shape[1:]
    return pl.pallas_call(
        functools.partial(grow_kernel, dims, ops_dev, parts, len(grounds)),
        out_shape=[
            jax.ShapeDtypeStruct((ops_dev, sec_dev, rows, columns), BF16),
            jax.ShapeDtypeStruct((sec_dev, columns, columns), BF16),
        ],
        in_specs=[SMEM] + [ANY] * len(grounds) + [VMEM] + [ANY] * len(pieces),
        out_specs=[ANY, VMEM],
        scratch_shapes=[
            pltpu.SMEM((3, LIST * len(parts)), jnp.int32),
            pltpu.VMEM((sec_dev // 2 * len(parts), rows, columns), BF16),
            pltpu.VMEM((DEPTH, rows, columns), BF16),
            pltpu.SemaphoreType.DMA((len(parts),)),
            pltpu.SemaphoreType.DMA((DEPTH,)),
            pltpu.SemaphoreType.DMA((4,)),
        ],
        compiler_params=pltpu.CompilerParams(vmem_limit_bytes=MEDIUM),
        cost_estimate=pl.CostEstimate(flops=1 << 20, bytes_accessed=1 << 12, transcendentals=0),
        name="grow",
    )(table, *grounds, op_matrices, *pieces)


def finish_kernel(dims, ops_dev, parts, table, *refs):
    ops, sectors, sec_dev, terms = dims
    grounds, (op_ref, env, _, out_ref, found, result, out_sem) = refs[: len(parts)], refs[len(parts) :]
    owner, core, spot = device_place()
    count_at = 2 * sec_dev * MIX_WIDTH
    list_at = count_at + 8
    total = jnp.int32(0)
    for n, (hops, h, sibling) in enumerate(parts):
        part = half_owner(owner, core, spot, hops, h, sibling)
        count = jnp.where(part >= 0, table[count_at + jnp.maximum(part, 0)], 0)

        def take(i, carry, part=part, total=total, n=n):
            entry = table[list_at + part * LIST + i]
            rest = entry // sec_dev
            found[0, total + i] = n
            found[1, total + i] = rest // ops_dev
            found[2, total + i] = lax.rem(rest, ops_dev)
            found[3, total + i] = lax.rem(entry, sec_dev)
            return carry

        lax.fori_loop(0, count, take, 0)
        total = total + count

    def drain(side):
        pltpu.make_async_copy(result.at[side], result.at[side], out_sem.at[side]).wait()

    def step(i, carry):
        side = lax.rem(i, DEPTH)
        which, s, o, local = (found[k, i] for k in range(4))
        block = grounds[0][s]
        for n in range(1, len(parts)):
            block = jnp.where(which == n, grounds[n][s], block)
        product = jnp.dot(block, op_ref[o], preferred_element_type=jnp.float32).astype(BF16)
        grown = jnp.dot(product, env[local], preferred_element_type=jnp.float32).astype(BF16)
        pl.when(i >= DEPTH)(lambda: drain(side))
        result[side] = grown
        pltpu.make_async_copy(result.at[side], out_ref.at[o, local], out_sem.at[side]).start()
        return carry

    lax.fori_loop(0, total, step, 0)
    for back in range(1, DEPTH + 1):
        pl.when(total >= back)(lambda back=back: drain(lax.rem(total - back, DEPTH)))


def finish(dims, table, parts, grounds, op_matrices, env, out, cost):
    ops, sectors, sec_dev, terms = dims
    ops_dev, _, rows, columns = out.shape
    return pl.pallas_call(
        functools.partial(finish_kernel, dims, ops_dev, parts),
        out_shape=jax.ShapeDtypeStruct(out.shape, BF16),
        in_specs=[SMEM] + [VMEM] * (len(parts) + 2) + [ANY],
        out_specs=ANY,
        scratch_shapes=[
            pltpu.SMEM((4, LIST * len(parts)), jnp.int32),
            pltpu.VMEM((DEPTH, rows, columns), BF16),
            pltpu.SemaphoreType.DMA((DEPTH,)),
        ],
        input_output_aliases={len(parts) + 3: 0},
        compiler_params=pltpu.CompilerParams(vmem_limit_bytes=MEDIUM),
        cost_estimate=pl.CostEstimate(flops=cost, bytes_accessed=1 << 12, transcendentals=0),
        name="finish",
    )(table, *grounds, op_matrices, env, out)


def line_of_four(ground_state, op_matrices, shift_map, new_slot, env_ground, env_src, env_coef):
    _, _, spot = device_place()
    sec_dev, rows, columns = ground_state.shape
    ops, sectors = shift_map.shape
    ops_dev = op_matrices.shape[0]
    dims = (ops, sectors, sec_dev, env_src.shape[1])
    half = rows // 2

    def stream(steps):
        up = [(2 * a, 2 * a + 2) for a in steps]
        down = [(2 * (3 - a) + 1, 2 * (2 - a) + 1) for a in steps]
        return lambda block: lax.ppermute(block, ("sec", "op"), up + down)

    def hand(block, spots):
        pairs_of = [(2 * z + core, 2 * z + 1 - core) for spot in spots for z, core in at[spot]]
        return lax.ppermute(block, ("sec", "op"), pairs_of)

    def across(block):
        leads = at[2] + at[3]
        pairs_of = [((z * 2 + x) * 2 + core, (z * 2 + 1 - x) * 2 + 1 - core) for z, core in leads for x in range(2)]
        return lax.ppermute(block, ("sec", "blk", "op"), pairs_of)

    def after(block, *others):
        return lax.optimization_barrier((block, *others))[0]

    at = [[(0, 0), (3, 1)], [(1, 0), (2, 1)], [(2, 0), (1, 1)], [(3, 0), (0, 1)]]
    every, middle, late, last = stream([0, 1, 2]), stream([1]), stream([1, 2]), stream([2])
    ground_half = ground_state.reshape(2, sec_dev, half, columns)
    both = range(2)

    sent0 = [head(h, env_ground, ground_half) for h in both]
    got0 = [every(sent0[h]) for h in both]
    got2 = [middle(got0[h]) for h in both]
    swapped0 = [hand(got0[h], [1, 3]) for h in both]
    table = tables(dims, ops_dev, shift_map, new_slot, env_src.T)
    sent4, made = zip(
        *[blend(dims, h, table, env_coef.T, got2[h], got0[h], env_ground, swapped0[h], ground_half) for h in both]
    )
    got4 = [every(sent4[h]) for h in both]
    near = [hand(made[h], [2]) for h in both]
    got6 = [late(got4[0]), late(after(got4[1], *near))]
    swapped4 = [hand(got4[h], [1, 2, 3]) for h in both]
    swapped6 = [hand(got6[0], [2, 3])]
    far = [across(jnp.where(spot == 2, made[h], got4[h])) for h in both]
    back = [hand(after(far[h], got6[0]), [0, 1]) for h in both]
    got8 = [last(got6[0]), last(after(got6[1], *swapped4, swapped6[0], back[0]))]
    pieces = [block[h] for h in both for block in (made, near, got4, swapped4, far, back)]

    parts = [(0, None, h, False, h * sec_dev // 2) for h in both]
    arrays = [ground_state]

    def blocks(block):
        return block.reshape(sec_dev // 2, rows, columns)

    def hold(mine, theirs, hops, h):
        for block, sibling in ((mine, False), (theirs, True)):
            parts.append((len(arrays), hops, h, sibling, 0))
            arrays.append(blocks(block))

    for h in both:
        hold(got0[h], swapped0[h], [0, 0, 0, 1], h)
        hold(got4[h], swapped4[h], [0, 1, 1, 0], h)
    hold(got6[0], swapped6[0], [0, 0, 2, 2], 0)
    parts.append((len(arrays), [0, 0, 2, 2], 1, False, 0))
    arrays.append(blocks(got6[1]))
    out, env = grow(dims, table, parts, arrays, op_matrices, pieces)
    swapped6.append(hand(after(got6[1], out), [2, 3]))
    swapped8 = [hand(after(got8[h], out), [3]) for h in both]
    ends, owners = [blocks(swapped6[1])], [([0, 0, 2, 2], 1, True)]
    for h in both:
        ends += [blocks(got8[h]), blocks(swapped8[h])]
        owners += [([0, 0, 0, 3], h, False), ([0, 0, 0, 3], h, True)]
        out = finish(dims, table, owners, ends, op_matrices, env, out, 1 << 20)
        ends, owners = [], []
    return out


def solution(mesh):
    four = mesh.shape["sec"] == 4 and mesh.shape["blk"] == 2 and mesh.shape["op"] == 2
    return jax.shard_map(
        line_of_four if four else whole_gather,
        mesh=mesh,
        in_specs=(
            P(("grp", "sec"), "blk", None),
            P(("grp", "op"), None, None),
            P("grp", None),
            P("grp"),
            P(("grp", "sec"), "blk", None),
            P("grp", None),
            P("grp", None),
        ),
        out_specs=P(("grp", "op"), "sec", "blk", None),
        check_vma=False,
    )
```

```python
import functools

import jax
import jax.numpy as jnp
from jax import lax
from jax.experimental import pallas as pl
from jax.experimental.pallas import tpu as pltpu
from jax.sharding import PartitionSpec as P

ANY = pl.BlockSpec(memory_space=pl.ANY)
HBM = pl.BlockSpec(memory_space=pltpu.HBM)
SMEM = pl.BlockSpec(memory_space=pltpu.SMEM)
VMEM = pl.BlockSpec(memory_space=pltpu.VMEM)
BF16 = jnp.bfloat16
LIMIT = 40 << 20
LARGE = 60 << 20
MEDIUM = 28 << 20


def mix_kernel(dims, picks, places, rows_at, ints, coef, *refs):
    ops, sectors, sec_dev, terms = dims
    count = len(picks)
    sources, refs = refs[:count], refs[count:]
    other = None
    if rows_at is not None:
        other, refs = refs[0], refs[1:]
    outs, (inverse, held, sems) = refs[: len(places)], refs[len(places) :]
    slot_at = ops * sectors
    src_at = slot_at + sectors
    pos_at = src_at + sectors * terms
    busy = ints[pos_at + 2] == 1

    def compute():
        def invert(t, carry):
            inverse[ints[slot_at + t]] = t
            return carry

        lax.fori_loop(0, sectors, invert, 0)

        def copies(place, i, side, act):
            owner = ints[pos_at + place]
            t = inverse[owner * sec_dev + i]
            for k in range(terms):
                source = ints[src_at + t * terms + k]
                if count == 1:
                    act(pltpu.make_async_copy(sources[0].at[source], held.at[side, k], sems.at[side, k]))
                    continue
                code = ints[pos_at + 16 + source // sec_dev]
                for q in range(count):

                    @pl.when(code == q)
                    def _(q=q, k=k, source=source):
                        src = sources[q].at[source % sec_dev]
                        if picks[q] is not None:
                            src = src.at[pl.ds(picks[q], held.shape[2])]
                        act(pltpu.make_async_copy(src, held.at[side, k], sems.at[side, k]))

        steps = [(n, place) for n, place in enumerate(places)]
        for n, place in steps:
            copies(place, 0, 0, lambda c: c.start())

            def step(i, carry, n=n, place=place):
                side = lax.rem(i, 2)

                @pl.when(i + 1 < sec_dev)
                def _():
                    copies(place, i + 1, 1 - side, lambda c: c.start())

                for k in range(terms):
                    pltpu.make_async_copy(held.at[side, k], held.at[side, k], sems.at[side, k]).wait()
                t = inverse[ints[pos_at + place] * sec_dev + i]
                height = min(32, held.shape[2])
                for r in range(0, held.shape[2], height):
                    total = coef[t * terms] * held[side, 0, r : r + height].astype(jnp.float32)
                    for k in range(1, terms):
                        total += coef[t * terms + k] * held[side, k, r : r + height].astype(jnp.float32)
                    outs[n][i, r : r + height] = total.astype(BF16)
                return carry

            lax.fori_loop(0, sec_dev, step, 0)

    if other is None:
        compute()
        return
    pl.when(busy)(compute)

    @pl.when(jnp.logical_not(busy))
    def _():
        copy = pltpu.make_async_copy(other.at[rows_at], outs[0], sems.at[0, 0])
        copy.start()
        copy.wait()


def mix(dims, ints, coef, sources, picks, places, height, other=None, rows_at=None):
    ops, sectors, sec_dev, terms = dims
    columns = sources[0].shape[-1]
    block = jax.ShapeDtypeStruct((sec_dev, height, columns), BF16)
    args = [ints, coef, *sources] + ([] if other is None else [other])
    return pl.pallas_call(
        functools.partial(mix_kernel, dims, picks, places, rows_at),
        out_shape=[block] * len(places),
        in_specs=[SMEM, SMEM] + [ANY] * (len(args) - 2),
        out_specs=[VMEM] * len(places),
        scratch_shapes=[
            pltpu.SMEM((sectors,), jnp.int32),
            pltpu.VMEM((2, terms, height, columns), BF16),
            pltpu.SemaphoreType.DMA((2, terms)),
        ],
        compiler_params=pltpu.CompilerParams(vmem_limit_bytes=LIMIT),
        cost_estimate=pl.CostEstimate(
            flops=2 * terms * len(places) * sec_dev * height * columns,
            bytes_accessed=2 * (terms + 1) * len(places) * sec_dev * height * columns,
            transcendentals=0,
        ),
        name="mix",
    )(*args)


def pair_kernel(dims, ops_dev, counts, pieces, first, ints, where, *refs):
    ops, sectors, sec_dev, terms = dims
    grounds, refs = refs[: len(counts)], refs[len(counts) :]
    op_ref, refs = refs[0], refs[1:]
    env_refs, refs = refs[:pieces], refs[pieces:]
    if not first:
        refs = refs[1:]
    out_ref, found, env, ground, result, env_sem, ground_sem, out_sem = refs
    slot_at = ops * sectors
    pos_at = slot_at + sectors + sectors * terms
    me = ints[pos_at]
    op_base = ints[pos_at + 3] * ops_dev
    env_copies = []
    for n in range(pieces):
        start = pl.multiple_of(where[len(counts) + n], 64)
        env_copies.append(
            pltpu.make_async_copy(env_refs[n], env.at[:, pl.ds(start, env_refs[n].shape[1])], env_sem.at[n])
        )
        env_copies[-1].start()

    def search(n, total):
        base = where[n]

        def candidate(s, total):
            for o in range(ops_dev):
                slot = ints[slot_at + ints[(op_base + o) * sectors + base + s]]
                local = slot - me * sec_dev
                mine = jnp.logical_and(local >= 0, local < sec_dev)
                found[0, total] = n
                found[1, total] = s
                found[2, total] = o
                found[3, total] = local
                total = total + mine.astype(jnp.int32)
            return total

        return lax.fori_loop(0, jnp.where(base >= 0, counts[n], 0), candidate, total)

    total = jnp.int32(0)
    for n in range(len(counts)):
        total = search(n, total)

    def fetch(i, side):
        for n in range(len(counts)):

            @pl.when(found[0, i] == n)
            def _(n=n):
                pltpu.make_async_copy(grounds[n].at[found[1, i]], ground.at[side], ground_sem.at[side]).start()

    @pl.when(total > 0)
    def _():
        fetch(0, 0)

    for copy in env_copies:
        copy.wait()

    def step(i, carry):
        side = lax.rem(i, 2)

        @pl.when(i + 1 < total)
        def _():
            fetch(i + 1, 1 - side)

        pltpu.make_async_copy(ground.at[side], ground.at[side], ground_sem.at[side]).wait()
        o, local = found[2, i], found[3, i]
        product = jnp.dot(ground[side], op_ref[o], preferred_element_type=jnp.float32).astype(BF16)
        grown = jnp.dot(product, env[local], preferred_element_type=jnp.float32).astype(BF16)

        @pl.when(i >= 2)
        def _():
            pltpu.make_async_copy(result.at[side], result.at[side], out_sem.at[side]).wait()

        result[side] = grown
        pltpu.make_async_copy(result.at[side], out_ref.at[o, local], out_sem.at[side]).start()
        return carry

    lax.fori_loop(0, total, step, 0)
    for back in (1, 2):

        @pl.when(total >= back)
        def _(back=back):
            side = lax.rem(total - back, 2)
            pltpu.make_async_copy(result.at[side], result.at[side], out_sem.at[side]).wait()


def pairs(dims, ints, where, grounds, op_matrices, env_pieces, out):
    ops, sectors, sec_dev, terms = dims
    ops_dev = op_matrices.shape[0]
    rows, columns = grounds[0].shape[1:]
    counts = [g.shape[0] for g in grounds]
    shape = jax.ShapeDtypeStruct((ops_dev, sec_dev, rows, columns), BF16)
    args = [ints, where, *grounds, op_matrices, *env_pieces] + ([] if out is None else [out])
    work = max(1, sum(counts) * ops_dev * sec_dev // sectors)
    return pl.pallas_call(
        functools.partial(pair_kernel, dims, ops_dev, counts, len(env_pieces), out is None),
        out_shape=shape,
        in_specs=[SMEM, SMEM] + [ANY] * len(grounds) + [VMEM] + [ANY] * (len(args) - 3 - len(grounds)),
        out_specs=ANY,
        scratch_shapes=[
            pltpu.SMEM((4, sum(counts) * ops_dev + 8), jnp.int32),
            pltpu.VMEM((sec_dev, columns, columns), BF16),
            pltpu.VMEM((2, rows, columns), BF16),
            pltpu.VMEM((2, rows, columns), BF16),
            pltpu.SemaphoreType.DMA((len(env_pieces),)),
            pltpu.SemaphoreType.DMA((2,)),
            pltpu.SemaphoreType.DMA((2,)),
        ],
        input_output_aliases={} if out is None else {len(args) - 1: 0},
        compiler_params=pltpu.CompilerParams(vmem_limit_bytes=LIMIT),
        cost_estimate=pl.CostEstimate(
            flops=4 * work * rows * columns * columns,
            bytes_accessed=2 * (2 * work * rows * columns + (ops_dev + sec_dev) * columns * columns),
            transcendentals=0,
        ),
        name="pairs",
    )(*args)


def pack(shift_map, new_slot, env_src, position):
    return jnp.concatenate(
        [shift_map.reshape(-1), new_slot, env_src.reshape(-1), jnp.stack(position).astype(jnp.int32)]
    )


def whole_gather(ground_state, op_matrices, shift_map, new_slot, env_ground, env_src, env_coef):
    owner = lax.axis_index("sec")
    group = lax.axis_index("op")
    halves = lax.axis_size("op")
    sec_dev, rows, columns = ground_state.shape
    ops, sectors = shift_map.shape
    dims = (ops, sectors, sec_dev, env_src.shape[1])
    zero = jnp.zeros((), jnp.int32)
    ints = pack(shift_map, new_slot, env_src, [owner, zero, zero + 1, group])

    def gather(blocks):
        part = rows // halves
        mine = lax.dynamic_slice_in_dim(blocks, group * part, part, 1)
        whole = lax.all_gather(lax.all_gather(mine, "sec", axis=0, tiled=True), "op", axis=1, tiled=True)
        return whole

    env_all = gather(env_ground)
    (env_new,) = mix(dims, ints, env_coef.reshape(-1), [env_all], [None], [0], rows)
    env_rows = lax.all_gather(env_new, "blk", axis=1, tiled=True)
    where = jnp.zeros((2,), jnp.int32)
    return pairs(dims, ints, where, [gather(ground_state)], op_matrices, [env_rows], None)


DEPTH = 4
MIX_WIDTH = 8
LIST = 16


def device_place():
    owner, core = lax.axis_index("sec"), lax.axis_index("op")
    return owner, core, jnp.where(core == 0, owner, 3 - owner)


def by_spot(spot, values):
    result = jnp.int32(values[0])
    for n in range(1, 4):
        result = jnp.where(spot == n, values[n], result)
    return result


def head_kernel(h, env, ground, sent, sem):
    _, _, spot = device_place()
    half = env.shape[1] // 2

    def send(source):
        copy = pltpu.make_async_copy(source, sent, sem)
        copy.start()
        copy.wait()

    pl.when(spot == 2)(lambda: send(ground.at[h]))
    pl.when(spot != 2)(lambda: send(env.at[:, pl.ds(h * half, half)]))


def head(h, env_ground, ground_half):
    sec_dev, rows, columns = env_ground.shape
    return pl.pallas_call(
        functools.partial(head_kernel, h),
        out_shape=jax.ShapeDtypeStruct((sec_dev, rows // 2, columns), BF16),
        in_specs=[HBM, HBM],
        out_specs=VMEM,
        scratch_shapes=[pltpu.SemaphoreType.DMA],
        compiler_params=pltpu.CompilerParams(vmem_limit_bytes=LARGE),
        cost_estimate=pl.CostEstimate(flops=0, bytes_accessed=2 * sec_dev * rows * columns, transcendentals=0),
        name="head",
    )(env_ground, ground_half)


def tables_kernel(dims, ops_dev, shift, slot, src, table, inverse):
    ops, sectors, sec_dev, terms = dims
    owner, core, _ = device_place()
    ahead = jnp.where(core == 0, jnp.minimum(owner + 1, 3), jnp.maximum(owner - 1, 0))

    def invert(t, carry):
        inverse[slot[t]] = t
        return carry

    lax.fori_loop(0, sectors, invert, 0)

    def terms_of(i, carry):
        place = jnp.where(i < sec_dev, ahead * sec_dev + i, owner * sec_dev + i - sec_dev)
        t = inverse[place]
        table[i * MIX_WIDTH] = t
        for k in range(terms):
            source = src[k, t]
            from_owner = source // sec_dev
            table[i * MIX_WIDTH + 1 + 2 * k] = jnp.where(core == 0, from_owner, 3 - from_owner)
            table[i * MIX_WIDTH + 2 + 2 * k] = source - from_owner * sec_dev
        return carry

    lax.fori_loop(0, 2 * sec_dev, terms_of, 0)
    count_at = 2 * sec_dev * MIX_WIDTH
    list_at = count_at + 8
    width = sec_dev // 2

    def pairs_of(n, carry):
        total = jnp.int32(0)
        for s in range(width):
            for o in range(ops_dev):
                local = slot[shift[core * ops_dev + o, n * width + s]] - owner * sec_dev
                table[list_at + n * LIST + total] = (s * ops_dev + o) * sec_dev + local
                total = total + jnp.logical_and(local >= 0, local < sec_dev).astype(jnp.int32)
        table[count_at + n] = total
        return carry

    lax.fori_loop(0, sectors // width, pairs_of, 0)


def tables(dims, ops_dev, shift_map, new_slot, env_src):
    ops, sectors, sec_dev, terms = dims
    return pl.pallas_call(
        functools.partial(tables_kernel, dims, ops_dev),
        out_shape=jax.ShapeDtypeStruct((2 * sec_dev * MIX_WIDTH + 8 + 8 * LIST,), jnp.int32),
        in_specs=[SMEM, SMEM, SMEM],
        out_specs=SMEM,
        scratch_shapes=[pltpu.SMEM((sectors,), jnp.int32)],
        cost_estimate=pl.CostEstimate(flops=10000, bytes_accessed=4000, transcendentals=0),
        name="tables",
    )(shift_map, new_slot, env_src)


def blend_kernel(dims, which, table, coef, second, first, env, other, ground, passed, made, held, sems):
    ops, sectors, sec_dev, terms = dims
    _, _, spot = device_place()
    height = held.shape[2]
    sources = [second, first, env.at[:, pl.ds(which * height, height)], other]

    @pl.when(spot == 2)
    def _():
        def fetch(i, carry):
            for k in range(terms):
                code, block = table[i * MIX_WIDTH + 1 + 2 * k], table[i * MIX_WIDTH + 2 + 2 * k]
                for q in range(4):

                    @pl.when(code == q)
                    def _(q=q, k=k, block=block):
                        pltpu.make_async_copy(sources[q].at[block], held.at[i, k], sems.at[i]).start()

            return carry

        lax.fori_loop(0, 2 * sec_dev, fetch, 0)

        def sums(out, lead):
            def one(i, carry):
                at = i + lead
                pltpu.make_async_copy(held.at[at], held.at[at], sems.at[at]).wait()
                t = table[at * MIX_WIDTH]
                weights = [coef[k, t] for k in range(terms)]
                for r in range(0, height, 32):
                    total = weights[0] * held[at, 0, r : r + 32].astype(jnp.float32)
                    for k in range(1, terms):
                        total += weights[k] * held[at, k, r : r + 32].astype(jnp.float32)
                    out[i, r : r + 32] = total.astype(BF16)
                return carry

            lax.fori_loop(0, sec_dev, one, 0)

        sums(passed, 0)
        sums(made, sec_dev)

    @pl.when(spot != 2)
    def _():
        copy = pltpu.make_async_copy(ground.at[which], passed, sems.at[0])
        copy.start()
        copy.wait()


def blend(dims, which, table, coef, second, first, env_ground, other, ground_half):
    ops, sectors, sec_dev, terms = dims
    block = jax.ShapeDtypeStruct(first.shape, BF16)
    _, height, columns = first.shape
    return pl.pallas_call(
        functools.partial(blend_kernel, dims, which),
        out_shape=[block, block],
        in_specs=[SMEM, SMEM] + [HBM] * 5,
        out_specs=[VMEM, VMEM],
        scratch_shapes=[
            pltpu.VMEM((2 * sec_dev, terms, height, columns), BF16),
            pltpu.SemaphoreType.DMA((2 * sec_dev,)),
        ],
        compiler_params=pltpu.CompilerParams(vmem_limit_bytes=MEDIUM),
        cost_estimate=pl.CostEstimate(
            flops=4 * terms * sec_dev * height * columns,
            bytes_accessed=4 * (terms + 1) * sec_dev * height * columns,
            transcendentals=0,
        ),
        name="blend",
    )(table, coef, second, first, env_ground, other, ground_half)


def half_owner(owner, core, spot, hops, h, sibling):
    if hops is None:
        return 2 * owner + h
    n = by_spot(3 - spot if sibling else spot, hops)
    back = jnp.where(core == 0, -1, 1) * (-1 if sibling else 1)
    return jnp.where(n > 0, 2 * (owner + back * n) + h, -1)


def grow_kernel(dims, ops_dev, parts, arrays, table, *refs):
    ops, sectors, sec_dev, terms = dims
    grounds, op_ref, refs = refs[:arrays], refs[arrays], refs[arrays + 1 :]
    owner, core, spot = device_place()
    rows, columns = grounds[0].shape[1:]
    width = sec_dev // 2
    pieces, (out_ref, env, found, ground, result, ground_sem, out_sem, env_sem) = refs[:12], refs[12:]
    count_at = 2 * sec_dev * MIX_WIDTH
    list_at = count_at + 8
    part_of = [half_owner(owner, core, spot, hops, h, sibling) for _, hops, h, sibling, _ in parts]
    for m, (n, _, _, _, lead) in enumerate(parts):

        @pl.when(part_of[m] >= 0)
        def _(m=m, n=n, lead=lead):
            source = grounds[n].at[pl.ds(lead, width)]
            pltpu.make_async_copy(source, ground.at[pl.ds(m * width, width)], ground_sem.at[m]).start()

    env_copies = []
    half = rows // 2
    own = lax.axis_index("blk") * rows
    for h in range(2):
        made, near, got, swapped, far, back = pieces[6 * h : 6 * h + 6]
        choices = [[swapped, near, made, got], [far, far, back, back]]
        for n, start in enumerate((own + h * half, rows - own + h * half)):
            target = env.at[:, pl.ds(pl.multiple_of(start, half), half)]
            for q in range(4):

                @pl.when(spot == q)
                def _(source=choices[n][q], target=target, sem=env_sem.at[2 * h + n]):
                    pltpu.make_async_copy(source, target, sem).start()

            env_copies.append(pltpu.make_async_copy(target, target, env_sem.at[2 * h + n]))

    total = jnp.int32(0)
    for m in range(len(parts)):
        part = part_of[m]
        count = jnp.where(part >= 0, table[count_at + jnp.maximum(part, 0)], 0)

        def take(i, carry, total=total, part=part, m=m):
            entry = table[list_at + part * LIST + i]
            rest = entry // sec_dev
            found[0, total + i] = m * width + rest // ops_dev
            found[1, total + i] = lax.rem(rest, ops_dev)
            found[2, total + i] = lax.rem(entry, sec_dev)
            return carry

        lax.fori_loop(0, count, take, 0)
        total = total + count
    for copy in env_copies:
        copy.wait()
    for m in range(len(parts)):

        @pl.when(part_of[m] >= 0)
        def _(m=m):
            here = ground.at[pl.ds(m * width, width)]
            pltpu.make_async_copy(here, here, ground_sem.at[m]).wait()

    def drain(side):
        pltpu.make_async_copy(result.at[side], result.at[side], out_sem.at[side]).wait()

    def step(i, carry):
        side = lax.rem(i, DEPTH)
        o, local = found[1, i], found[2, i]
        product = jnp.dot(ground[found[0, i]], op_ref[o], preferred_element_type=jnp.float32).astype(BF16)
        grown = jnp.dot(product, env[local], preferred_element_type=jnp.float32).astype(BF16)
        pl.when(i >= DEPTH)(lambda: drain(side))
        result[side] = grown
        pltpu.make_async_copy(result.at[side], out_ref.at[o, local], out_sem.at[side]).start()
        return carry

    lax.fori_loop(0, total, step, 0)
    for back in range(1, DEPTH + 1):
        pl.when(total >= back)(lambda back=back: drain(lax.rem(total - back, DEPTH)))


def grow(dims, table, parts, grounds, op_matrices, pieces):
    ops, sectors, sec_dev, terms = dims
    ops_dev = op_matrices.shape[0]
    rows, columns = grounds[0].shape[1:]
    return pl.pallas_call(
        functools.partial(grow_kernel, dims, ops_dev, parts, len(grounds)),
        out_shape=[
            jax.ShapeDtypeStruct((ops_dev, sec_dev, rows, columns), BF16),
            jax.ShapeDtypeStruct((sec_dev, columns, columns), BF16),
        ],
        in_specs=[SMEM] + [ANY] * len(grounds) + [VMEM] + [ANY] * len(pieces),
        out_specs=[ANY, VMEM],
        scratch_shapes=[
            pltpu.SMEM((3, LIST * len(parts)), jnp.int32),
            pltpu.VMEM((sec_dev // 2 * len(parts), rows, columns), BF16),
            pltpu.VMEM((DEPTH, rows, columns), BF16),
            pltpu.SemaphoreType.DMA((len(parts),)),
            pltpu.SemaphoreType.DMA((DEPTH,)),
            pltpu.SemaphoreType.DMA((4,)),
        ],
        compiler_params=pltpu.CompilerParams(vmem_limit_bytes=MEDIUM),
        cost_estimate=pl.CostEstimate(flops=1 << 20, bytes_accessed=1 << 12, transcendentals=0),
        name="grow",
    )(table, *grounds, op_matrices, *pieces)


def finish_kernel(dims, ops_dev, parts, table, *refs):
    ops, sectors, sec_dev, terms = dims
    grounds, (op_ref, env, _, out_ref, found, result, out_sem) = refs[: len(parts)], refs[len(parts) :]
    owner, core, spot = device_place()
    count_at = 2 * sec_dev * MIX_WIDTH
    list_at = count_at + 8
    total = jnp.int32(0)
    for n, (hops, h, sibling) in enumerate(parts):
        part = half_owner(owner, core, spot, hops, h, sibling)
        count = jnp.where(part >= 0, table[count_at + jnp.maximum(part, 0)], 0)

        def take(i, carry, part=part, total=total, n=n):
            entry = table[list_at + part * LIST + i]
            rest = entry // sec_dev
            found[0, total + i] = n
            found[1, total + i] = rest // ops_dev
            found[2, total + i] = lax.rem(rest, ops_dev)
            found[3, total + i] = lax.rem(entry, sec_dev)
            return carry

        lax.fori_loop(0, count, take, 0)
        total = total + count

    def drain(side):
        pltpu.make_async_copy(result.at[side], result.at[side], out_sem.at[side]).wait()

    def step(i, carry):
        side = lax.rem(i, DEPTH)
        which, s, o, local = (found[k, i] for k in range(4))
        block = grounds[0][s]
        for n in range(1, len(parts)):
            block = jnp.where(which == n, grounds[n][s], block)
        product = jnp.dot(block, op_ref[o], preferred_element_type=jnp.float32).astype(BF16)
        grown = jnp.dot(product, env[local], preferred_element_type=jnp.float32).astype(BF16)
        pl.when(i >= DEPTH)(lambda: drain(side))
        result[side] = grown
        pltpu.make_async_copy(result.at[side], out_ref.at[o, local], out_sem.at[side]).start()
        return carry

    lax.fori_loop(0, total, step, 0)
    for back in range(1, DEPTH + 1):
        pl.when(total >= back)(lambda back=back: drain(lax.rem(total - back, DEPTH)))


def finish(dims, table, parts, grounds, op_matrices, env, out, cost):
    ops, sectors, sec_dev, terms = dims
    ops_dev, _, rows, columns = out.shape
    return pl.pallas_call(
        functools.partial(finish_kernel, dims, ops_dev, parts),
        out_shape=jax.ShapeDtypeStruct(out.shape, BF16),
        in_specs=[SMEM] + [VMEM] * (len(parts) + 2) + [ANY],
        out_specs=ANY,
        scratch_shapes=[
            pltpu.SMEM((4, LIST * len(parts)), jnp.int32),
            pltpu.VMEM((DEPTH, rows, columns), BF16),
            pltpu.SemaphoreType.DMA((DEPTH,)),
        ],
        input_output_aliases={len(parts) + 3: 0},
        compiler_params=pltpu.CompilerParams(vmem_limit_bytes=MEDIUM),
        cost_estimate=pl.CostEstimate(flops=cost, bytes_accessed=1 << 12, transcendentals=0),
        name="finish",
    )(table, *grounds, op_matrices, env, out)


def line_of_four(ground_state, op_matrices, shift_map, new_slot, env_ground, env_src, env_coef):
    _, _, spot = device_place()
    sec_dev, rows, columns = ground_state.shape
    ops, sectors = shift_map.shape
    ops_dev = op_matrices.shape[0]
    dims = (ops, sectors, sec_dev, env_src.shape[1])
    half = rows // 2

    def stream(steps):
        up = [(2 * a, 2 * a + 2) for a in steps]
        down = [(2 * (3 - a) + 1, 2 * (2 - a) + 1) for a in steps]
        return lambda block: lax.ppermute(block, ("sec", "op"), up + down)

    def hand(block, spots):
        pairs_of = [(2 * z + core, 2 * z + 1 - core) for spot in spots for z, core in at[spot]]
        return lax.ppermute(block, ("sec", "op"), pairs_of)

    def across(block):
        leads = at[2] + at[3]
        pairs_of = [((z * 2 + x) * 2 + core, (z * 2 + 1 - x) * 2 + 1 - core) for z, core in leads for x in range(2)]
        return lax.ppermute(block, ("sec", "blk", "op"), pairs_of)

    def after(block, *others):
        return lax.optimization_barrier((block, *others))[0]

    at = [[(0, 0), (3, 1)], [(1, 0), (2, 1)], [(2, 0), (1, 1)], [(3, 0), (0, 1)]]
    every, middle, late, last = stream([0, 1, 2]), stream([1]), stream([1, 2]), stream([2])
    ground_half = ground_state.reshape(2, sec_dev, half, columns)
    both = range(2)

    sent0 = [head(h, env_ground, ground_half) for h in both]
    got0 = [every(sent0[h]) for h in both]
    got2 = [middle(got0[h]) for h in both]
    swapped0 = [hand(got0[h], [1, 3]) for h in both]
    table = tables(dims, ops_dev, shift_map, new_slot, env_src.T)
    sent4, made = zip(
        *[blend(dims, h, table, env_coef.T, got2[h], got0[h], env_ground, swapped0[h], ground_half) for h in both]
    )
    got4 = [every(sent4[h]) for h in both]
    near = [hand(made[h], [2]) for h in both]
    got6 = [late(got4[0]), late(after(got4[1], *near))]
    swapped4 = [hand(got4[h], [1, 2, 3]) for h in both]
    far = [across(jnp.where(spot == 2, made[h], got4[h])) for h in both]
    back = [hand(after(far[h], got6[0]), [0, 1]) for h in both]
    got8 = [last(got6[0]), last(after(got6[1], *swapped4, back[0]))]
    pieces = [block[h] for h in both for block in (made, near, got4, swapped4, far, back)]

    parts = [(0, None, h, False, h * sec_dev // 2) for h in both]
    arrays = [ground_state]

    def blocks(block):
        return block.reshape(sec_dev // 2, rows, columns)

    def hold(mine, theirs, hops, h):
        for block, sibling in ((mine, False), (theirs, True)):
            parts.append((len(arrays), hops, h, sibling, 0))
            arrays.append(blocks(block))

    for h in both:
        hold(got0[h], swapped0[h], [0, 0, 0, 1], h)
        hold(got4[h], swapped4[h], [0, 1, 1, 0], h)
    for h in both:
        parts.append((len(arrays), [0, 0, 2, 2], h, False, 0))
        arrays.append(blocks(got6[h]))
    out, env = grow(dims, table, parts, arrays, op_matrices, pieces)
    swapped6 = [hand(after(got6[h], out), [2, 3]) for h in both]
    swapped8 = [hand(after(got8[h], out), [3]) for h in both]
    ends = [blocks(block) for block in swapped6]
    owners = [([0, 0, 2, 2], h, True) for h in both]
    for h in both:
        ends += [blocks(got8[h]), blocks(swapped8[h])]
        owners += [([0, 0, 0, 3], h, False), ([0, 0, 0, 3], h, True)]
        out = finish(dims, table, owners, ends, op_matrices, env, out, 1 << 20)
        ends, owners = [], []
    return out


def solution(mesh):
    four = mesh.shape["sec"] == 4 and mesh.shape["blk"] == 2 and mesh.shape["op"] == 2
    return jax.shard_map(
        line_of_four if four else whole_gather,
        mesh=mesh,
        in_specs=(
            P(("grp", "sec"), "blk", None),
            P(("grp", "op"), None, None),
            P("grp", None),
            P("grp"),
            P(("grp", "sec"), "blk", None),
            P("grp", None),
            P("grp", None),
        ),
        out_specs=P(("grp", "op"), "sec", "blk", None),
        check_vma=False,
    )
```

```python
import functools

import jax
import jax.numpy as jnp
from jax import lax
from jax.experimental import pallas as pl
from jax.experimental.pallas import tpu as pltpu
from jax.sharding import PartitionSpec as P

ANY = pl.BlockSpec(memory_space=pl.ANY)
HBM = pl.BlockSpec(memory_space=pltpu.HBM)
SMEM = pl.BlockSpec(memory_space=pltpu.SMEM)
VMEM = pl.BlockSpec(memory_space=pltpu.VMEM)
BF16 = jnp.bfloat16
LIMIT = 40 << 20
LARGE = 60 << 20
MEDIUM = 28 << 20


def mix_kernel(dims, picks, places, rows_at, ints, coef, *refs):
    ops, sectors, sec_dev, terms = dims
    count = len(picks)
    sources, refs = refs[:count], refs[count:]
    other = None
    if rows_at is not None:
        other, refs = refs[0], refs[1:]
    outs, (inverse, held, sems) = refs[: len(places)], refs[len(places) :]
    slot_at = ops * sectors
    src_at = slot_at + sectors
    pos_at = src_at + sectors * terms
    busy = ints[pos_at + 2] == 1

    def compute():
        def invert(t, carry):
            inverse[ints[slot_at + t]] = t
            return carry

        lax.fori_loop(0, sectors, invert, 0)

        def copies(place, i, side, act):
            owner = ints[pos_at + place]
            t = inverse[owner * sec_dev + i]
            for k in range(terms):
                source = ints[src_at + t * terms + k]
                if count == 1:
                    act(pltpu.make_async_copy(sources[0].at[source], held.at[side, k], sems.at[side, k]))
                    continue
                code = ints[pos_at + 16 + source // sec_dev]
                for q in range(count):

                    @pl.when(code == q)
                    def _(q=q, k=k, source=source):
                        src = sources[q].at[source % sec_dev]
                        if picks[q] is not None:
                            src = src.at[pl.ds(picks[q], held.shape[2])]
                        act(pltpu.make_async_copy(src, held.at[side, k], sems.at[side, k]))

        steps = [(n, place) for n, place in enumerate(places)]
        for n, place in steps:
            copies(place, 0, 0, lambda c: c.start())

            def step(i, carry, n=n, place=place):
                side = lax.rem(i, 2)

                @pl.when(i + 1 < sec_dev)
                def _():
                    copies(place, i + 1, 1 - side, lambda c: c.start())

                for k in range(terms):
                    pltpu.make_async_copy(held.at[side, k], held.at[side, k], sems.at[side, k]).wait()
                t = inverse[ints[pos_at + place] * sec_dev + i]
                height = min(32, held.shape[2])
                for r in range(0, held.shape[2], height):
                    total = coef[t * terms] * held[side, 0, r : r + height].astype(jnp.float32)
                    for k in range(1, terms):
                        total += coef[t * terms + k] * held[side, k, r : r + height].astype(jnp.float32)
                    outs[n][i, r : r + height] = total.astype(BF16)
                return carry

            lax.fori_loop(0, sec_dev, step, 0)

    if other is None:
        compute()
        return
    pl.when(busy)(compute)

    @pl.when(jnp.logical_not(busy))
    def _():
        copy = pltpu.make_async_copy(other.at[rows_at], outs[0], sems.at[0, 0])
        copy.start()
        copy.wait()


def mix(dims, ints, coef, sources, picks, places, height, other=None, rows_at=None):
    ops, sectors, sec_dev, terms = dims
    columns = sources[0].shape[-1]
    block = jax.ShapeDtypeStruct((sec_dev, height, columns), BF16)
    args = [ints, coef, *sources] + ([] if other is None else [other])
    return pl.pallas_call(
        functools.partial(mix_kernel, dims, picks, places, rows_at),
        out_shape=[block] * len(places),
        in_specs=[SMEM, SMEM] + [ANY] * (len(args) - 2),
        out_specs=[VMEM] * len(places),
        scratch_shapes=[
            pltpu.SMEM((sectors,), jnp.int32),
            pltpu.VMEM((2, terms, height, columns), BF16),
            pltpu.SemaphoreType.DMA((2, terms)),
        ],
        compiler_params=pltpu.CompilerParams(vmem_limit_bytes=LIMIT),
        cost_estimate=pl.CostEstimate(
            flops=2 * terms * len(places) * sec_dev * height * columns,
            bytes_accessed=2 * (terms + 1) * len(places) * sec_dev * height * columns,
            transcendentals=0,
        ),
        name="mix",
    )(*args)


def pair_kernel(dims, ops_dev, counts, pieces, first, ints, where, *refs):
    ops, sectors, sec_dev, terms = dims
    grounds, refs = refs[: len(counts)], refs[len(counts) :]
    op_ref, refs = refs[0], refs[1:]
    env_refs, refs = refs[:pieces], refs[pieces:]
    if not first:
        refs = refs[1:]
    out_ref, found, env, ground, result, env_sem, ground_sem, out_sem = refs
    slot_at = ops * sectors
    pos_at = slot_at + sectors + sectors * terms
    me = ints[pos_at]
    op_base = ints[pos_at + 3] * ops_dev
    env_copies = []
    for n in range(pieces):
        start = pl.multiple_of(where[len(counts) + n], 64)
        env_copies.append(
            pltpu.make_async_copy(env_refs[n], env.at[:, pl.ds(start, env_refs[n].shape[1])], env_sem.at[n])
        )
        env_copies[-1].start()

    def search(n, total):
        base = where[n]

        def candidate(s, total):
            for o in range(ops_dev):
                slot = ints[slot_at + ints[(op_base + o) * sectors + base + s]]
                local = slot - me * sec_dev
                mine = jnp.logical_and(local >= 0, local < sec_dev)
                found[0, total] = n
                found[1, total] = s
                found[2, total] = o
                found[3, total] = local
                total = total + mine.astype(jnp.int32)
            return total

        return lax.fori_loop(0, jnp.where(base >= 0, counts[n], 0), candidate, total)

    total = jnp.int32(0)
    for n in range(len(counts)):
        total = search(n, total)

    def fetch(i, side):
        for n in range(len(counts)):

            @pl.when(found[0, i] == n)
            def _(n=n):
                pltpu.make_async_copy(grounds[n].at[found[1, i]], ground.at[side], ground_sem.at[side]).start()

    @pl.when(total > 0)
    def _():
        fetch(0, 0)

    for copy in env_copies:
        copy.wait()

    def step(i, carry):
        side = lax.rem(i, 2)

        @pl.when(i + 1 < total)
        def _():
            fetch(i + 1, 1 - side)

        pltpu.make_async_copy(ground.at[side], ground.at[side], ground_sem.at[side]).wait()
        o, local = found[2, i], found[3, i]
        product = jnp.dot(ground[side], op_ref[o], preferred_element_type=jnp.float32).astype(BF16)
        grown = jnp.dot(product, env[local], preferred_element_type=jnp.float32).astype(BF16)

        @pl.when(i >= 2)
        def _():
            pltpu.make_async_copy(result.at[side], result.at[side], out_sem.at[side]).wait()

        result[side] = grown
        pltpu.make_async_copy(result.at[side], out_ref.at[o, local], out_sem.at[side]).start()
        return carry

    lax.fori_loop(0, total, step, 0)
    for back in (1, 2):

        @pl.when(total >= back)
        def _(back=back):
            side = lax.rem(total - back, 2)
            pltpu.make_async_copy(result.at[side], result.at[side], out_sem.at[side]).wait()


def pairs(dims, ints, where, grounds, op_matrices, env_pieces, out):
    ops, sectors, sec_dev, terms = dims
    ops_dev = op_matrices.shape[0]
    rows, columns = grounds[0].shape[1:]
    counts = [g.shape[0] for g in grounds]
    shape = jax.ShapeDtypeStruct((ops_dev, sec_dev, rows, columns), BF16)
    args = [ints, where, *grounds, op_matrices, *env_pieces] + ([] if out is None else [out])
    work = max(1, sum(counts) * ops_dev * sec_dev // sectors)
    return pl.pallas_call(
        functools.partial(pair_kernel, dims, ops_dev, counts, len(env_pieces), out is None),
        out_shape=shape,
        in_specs=[SMEM, SMEM] + [ANY] * len(grounds) + [VMEM] + [ANY] * (len(args) - 3 - len(grounds)),
        out_specs=ANY,
        scratch_shapes=[
            pltpu.SMEM((4, sum(counts) * ops_dev + 8), jnp.int32),
            pltpu.VMEM((sec_dev, columns, columns), BF16),
            pltpu.VMEM((2, rows, columns), BF16),
            pltpu.VMEM((2, rows, columns), BF16),
            pltpu.SemaphoreType.DMA((len(env_pieces),)),
            pltpu.SemaphoreType.DMA((2,)),
            pltpu.SemaphoreType.DMA((2,)),
        ],
        input_output_aliases={} if out is None else {len(args) - 1: 0},
        compiler_params=pltpu.CompilerParams(vmem_limit_bytes=LIMIT),
        cost_estimate=pl.CostEstimate(
            flops=4 * work * rows * columns * columns,
            bytes_accessed=2 * (2 * work * rows * columns + (ops_dev + sec_dev) * columns * columns),
            transcendentals=0,
        ),
        name="pairs",
    )(*args)


def pack(shift_map, new_slot, env_src, position):
    return jnp.concatenate(
        [shift_map.reshape(-1), new_slot, env_src.reshape(-1), jnp.stack(position).astype(jnp.int32)]
    )


def whole_gather(ground_state, op_matrices, shift_map, new_slot, env_ground, env_src, env_coef):
    owner = lax.axis_index("sec")
    group = lax.axis_index("op")
    halves = lax.axis_size("op")
    sec_dev, rows, columns = ground_state.shape
    ops, sectors = shift_map.shape
    dims = (ops, sectors, sec_dev, env_src.shape[1])
    zero = jnp.zeros((), jnp.int32)
    ints = pack(shift_map, new_slot, env_src, [owner, zero, zero + 1, group])

    def gather(blocks):
        part = rows // halves
        mine = lax.dynamic_slice_in_dim(blocks, group * part, part, 1)
        whole = lax.all_gather(lax.all_gather(mine, "sec", axis=0, tiled=True), "op", axis=1, tiled=True)
        return whole

    env_all = gather(env_ground)
    (env_new,) = mix(dims, ints, env_coef.reshape(-1), [env_all], [None], [0], rows)
    env_rows = lax.all_gather(env_new, "blk", axis=1, tiled=True)
    where = jnp.zeros((2,), jnp.int32)
    return pairs(dims, ints, where, [gather(ground_state)], op_matrices, [env_rows], None)


DEPTH = 4
MIX_WIDTH = 8
LIST = 16


def device_place():
    owner, core = lax.axis_index("sec"), lax.axis_index("op")
    return owner, core, jnp.where(core == 0, owner, 3 - owner)


def by_spot(spot, values):
    result = jnp.int32(values[0])
    for n in range(1, 4):
        result = jnp.where(spot == n, values[n], result)
    return result


def head_kernel(h, env, ground, sent, sem):
    _, _, spot = device_place()
    half = env.shape[1] // 2

    def send(source):
        copy = pltpu.make_async_copy(source, sent, sem)
        copy.start()
        copy.wait()

    pl.when(spot == 2)(lambda: send(ground.at[h]))
    pl.when(spot != 2)(lambda: send(env.at[:, pl.ds(h * half, half)]))


def head(h, env_ground, ground_half):
    sec_dev, rows, columns = env_ground.shape
    return pl.pallas_call(
        functools.partial(head_kernel, h),
        out_shape=jax.ShapeDtypeStruct((sec_dev, rows // 2, columns), BF16),
        in_specs=[HBM, HBM],
        out_specs=VMEM,
        scratch_shapes=[pltpu.SemaphoreType.DMA],
        compiler_params=pltpu.CompilerParams(vmem_limit_bytes=LARGE),
        cost_estimate=pl.CostEstimate(flops=0, bytes_accessed=2 * sec_dev * rows * columns, transcendentals=0),
        name="head",
    )(env_ground, ground_half)


def tables_kernel(dims, ops_dev, shift, slot, src, table, inverse):
    ops, sectors, sec_dev, terms = dims
    owner, core, _ = device_place()
    ahead = jnp.where(core == 0, jnp.minimum(owner + 1, 3), jnp.maximum(owner - 1, 0))

    def invert(t, carry):
        inverse[slot[t]] = t
        return carry

    lax.fori_loop(0, sectors, invert, 0)

    def terms_of(i, carry):
        place = jnp.where(i < sec_dev, ahead * sec_dev + i, owner * sec_dev + i - sec_dev)
        t = inverse[place]
        table[i * MIX_WIDTH] = t
        for k in range(terms):
            source = src[k, t]
            from_owner = source // sec_dev
            table[i * MIX_WIDTH + 1 + 2 * k] = jnp.where(core == 0, from_owner, 3 - from_owner)
            table[i * MIX_WIDTH + 2 + 2 * k] = source - from_owner * sec_dev
        return carry

    lax.fori_loop(0, 2 * sec_dev, terms_of, 0)
    count_at = 2 * sec_dev * MIX_WIDTH
    list_at = count_at + 8
    width = sec_dev // 2

    def pairs_of(n, carry):
        total = jnp.int32(0)
        for s in range(width):
            for o in range(ops_dev):
                local = slot[shift[core * ops_dev + o, n * width + s]] - owner * sec_dev
                table[list_at + n * LIST + total] = (s * ops_dev + o) * sec_dev + local
                total = total + jnp.logical_and(local >= 0, local < sec_dev).astype(jnp.int32)
        table[count_at + n] = total
        return carry

    lax.fori_loop(0, sectors // width, pairs_of, 0)


def tables(dims, ops_dev, shift_map, new_slot, env_src):
    ops, sectors, sec_dev, terms = dims
    return pl.pallas_call(
        functools.partial(tables_kernel, dims, ops_dev),
        out_shape=jax.ShapeDtypeStruct((2 * sec_dev * MIX_WIDTH + 8 + 8 * LIST,), jnp.int32),
        in_specs=[SMEM, SMEM, SMEM],
        out_specs=SMEM,
        scratch_shapes=[pltpu.SMEM((sectors,), jnp.int32)],
        cost_estimate=pl.CostEstimate(flops=10000, bytes_accessed=4000, transcendentals=0),
        name="tables",
    )(shift_map, new_slot, env_src)


def blend_kernel(dims, which, table, coef, second, first, env, other, ground, passed, made, held, sems):
    ops, sectors, sec_dev, terms = dims
    _, _, spot = device_place()
    height = held.shape[2]
    sources = [second, first, env.at[:, pl.ds(which * height, height)], other]

    @pl.when(spot == 2)
    def _():
        def fetch(i, carry):
            for k in range(terms):
                code, block = table[i * MIX_WIDTH + 1 + 2 * k], table[i * MIX_WIDTH + 2 + 2 * k]
                for q in range(4):

                    @pl.when(code == q)
                    def _(q=q, k=k, block=block):
                        pltpu.make_async_copy(sources[q].at[block], held.at[i, k], sems.at[i]).start()

            return carry

        lax.fori_loop(0, 2 * sec_dev, fetch, 0)

        def sums(out, lead):
            def one(i, carry):
                at = i + lead
                pltpu.make_async_copy(held.at[at], held.at[at], sems.at[at]).wait()
                t = table[at * MIX_WIDTH]
                weights = [coef[k, t] for k in range(terms)]
                for r in range(0, height, 32):
                    total = weights[0] * held[at, 0, r : r + 32].astype(jnp.float32)
                    for k in range(1, terms):
                        total += weights[k] * held[at, k, r : r + 32].astype(jnp.float32)
                    out[i, r : r + 32] = total.astype(BF16)
                return carry

            lax.fori_loop(0, sec_dev, one, 0)

        sums(passed, 0)
        sums(made, sec_dev)

    @pl.when(spot != 2)
    def _():
        copy = pltpu.make_async_copy(ground.at[which], passed, sems.at[0])
        copy.start()
        copy.wait()


def blend(dims, which, table, coef, second, first, env_ground, other, ground_half):
    ops, sectors, sec_dev, terms = dims
    block = jax.ShapeDtypeStruct(first.shape, BF16)
    _, height, columns = first.shape
    return pl.pallas_call(
        functools.partial(blend_kernel, dims, which),
        out_shape=[block, block],
        in_specs=[SMEM, SMEM] + [HBM] * 5,
        out_specs=[VMEM, VMEM],
        scratch_shapes=[
            pltpu.VMEM((2 * sec_dev, terms, height, columns), BF16),
            pltpu.SemaphoreType.DMA((2 * sec_dev,)),
        ],
        compiler_params=pltpu.CompilerParams(vmem_limit_bytes=MEDIUM),
        cost_estimate=pl.CostEstimate(
            flops=4 * terms * sec_dev * height * columns,
            bytes_accessed=4 * (terms + 1) * sec_dev * height * columns,
            transcendentals=0,
        ),
        name="blend",
    )(table, coef, second, first, env_ground, other, ground_half)


def half_owner(owner, core, spot, hops, h, sibling):
    if hops is None:
        return 2 * owner + h
    n = by_spot(3 - spot if sibling else spot, hops)
    back = jnp.where(core == 0, -1, 1) * (-1 if sibling else 1)
    return jnp.where(n > 0, 2 * (owner + back * n) + h, -1)


def grow_kernel(dims, ops_dev, parts, arrays, table, *refs):
    ops, sectors, sec_dev, terms = dims
    grounds, op_ref, refs = refs[:arrays], refs[arrays], refs[arrays + 1 :]
    owner, core, spot = device_place()
    rows, columns = grounds[0].shape[1:]
    width = sec_dev // 2
    pieces, (out_ref, env, found, ground, result, ground_sem, out_sem, env_sem) = refs[:12], refs[12:]
    count_at = 2 * sec_dev * MIX_WIDTH
    list_at = count_at + 8
    part_of = [half_owner(owner, core, spot, hops, h, sibling) for _, hops, h, sibling, _ in parts]
    for m, (n, _, _, _, lead) in enumerate(parts):

        @pl.when(part_of[m] >= 0)
        def _(m=m, n=n, lead=lead):
            source = grounds[n].at[pl.ds(lead, width)]
            pltpu.make_async_copy(source, ground.at[pl.ds(m * width, width)], ground_sem.at[m]).start()

    env_copies = []
    half = rows // 2
    own = lax.axis_index("blk") * rows
    for h in range(2):
        made, near, got, swapped, far, back = pieces[6 * h : 6 * h + 6]
        choices = [[swapped, near, made, got], [far, far, back, back]]
        for n, start in enumerate((own + h * half, rows - own + h * half)):
            target = env.at[:, pl.ds(pl.multiple_of(start, half), half)]
            for q in range(4):

                @pl.when(spot == q)
                def _(source=choices[n][q], target=target, sem=env_sem.at[2 * h + n]):
                    pltpu.make_async_copy(source, target, sem).start()

            env_copies.append(pltpu.make_async_copy(target, target, env_sem.at[2 * h + n]))

    total = jnp.int32(0)
    for m in range(len(parts)):
        part = part_of[m]
        count = jnp.where(part >= 0, table[count_at + jnp.maximum(part, 0)], 0)

        def take(i, carry, total=total, part=part, m=m):
            entry = table[list_at + part * LIST + i]
            rest = entry // sec_dev
            found[0, total + i] = m * width + rest // ops_dev
            found[1, total + i] = lax.rem(rest, ops_dev)
            found[2, total + i] = lax.rem(entry, sec_dev)
            return carry

        lax.fori_loop(0, count, take, 0)
        total = total + count
    for copy in env_copies:
        copy.wait()
    for m in range(len(parts)):

        @pl.when(part_of[m] >= 0)
        def _(m=m):
            here = ground.at[pl.ds(m * width, width)]
            pltpu.make_async_copy(here, here, ground_sem.at[m]).wait()

    def drain(side):
        pltpu.make_async_copy(result.at[side], result.at[side], out_sem.at[side]).wait()

    def grown_of(i):
        o, local = found[1, i], found[2, i]
        block = ground[found[0, i]]
        product = jnp.dot(block, op_ref[o], preferred_element_type=jnp.float32).astype(BF16)
        return jnp.dot(product, env[local], preferred_element_type=jnp.float32).astype(BF16)

    def send(i):
        side = lax.rem(i, DEPTH)
        target = out_ref.at[found[1, i], found[2, i]]
        pltpu.make_async_copy(result.at[side], target, out_sem.at[side]).start()

    def step(n, carry):
        i, j = 2 * n, 2 * n + 1
        values = grown_of(i), grown_of(jnp.minimum(j, total - 1))

        @pl.when(n >= 2)
        def _():
            drain(lax.rem(i, DEPTH))
            drain(lax.rem(j, DEPTH))

        result[lax.rem(i, DEPTH)] = values[0]
        result[lax.rem(j, DEPTH)] = values[1]
        send(i)
        pl.when(j < total)(lambda: send(j))
        return carry

    steps = (total + 1) // 2
    lax.fori_loop(0, steps, step, 0)
    left = total - 2 * jnp.maximum(steps - 2, 0)
    for back in range(1, DEPTH + 1):
        pl.when(left >= back)(lambda back=back: drain(lax.rem(total - back, DEPTH)))


def grow(dims, table, parts, grounds, op_matrices, pieces):
    ops, sectors, sec_dev, terms = dims
    ops_dev = op_matrices.shape[0]
    rows, columns = grounds[0].shape[1:]
    return pl.pallas_call(
        functools.partial(grow_kernel, dims, ops_dev, parts, len(grounds)),
        out_shape=[
            jax.ShapeDtypeStruct((ops_dev, sec_dev, rows, columns), BF16),
            jax.ShapeDtypeStruct((sec_dev, columns, columns), BF16),
        ],
        in_specs=[SMEM] + [ANY] * len(grounds) + [VMEM] + [ANY] * len(pieces),
        out_specs=[ANY, VMEM],
        scratch_shapes=[
            pltpu.SMEM((3, LIST * len(parts)), jnp.int32),
            pltpu.VMEM((sec_dev // 2 * len(parts), rows, columns), BF16),
            pltpu.VMEM((DEPTH, rows, columns), BF16),
            pltpu.SemaphoreType.DMA((len(parts),)),
            pltpu.SemaphoreType.DMA((DEPTH,)),
            pltpu.SemaphoreType.DMA((4,)),
        ],
        compiler_params=pltpu.CompilerParams(vmem_limit_bytes=MEDIUM),
        cost_estimate=pl.CostEstimate(flops=1 << 20, bytes_accessed=1 << 12, transcendentals=0),
        name="grow",
    )(table, *grounds, op_matrices, *pieces)


def finish_kernel(dims, ops_dev, parts, table, *refs):
    ops, sectors, sec_dev, terms = dims
    grounds, (op_ref, env, _, out_ref, found, result, out_sem) = refs[: len(parts)], refs[len(parts) :]
    owner, core, spot = device_place()
    count_at = 2 * sec_dev * MIX_WIDTH
    list_at = count_at + 8
    total = jnp.int32(0)
    for n, (hops, h, sibling) in enumerate(parts):
        part = half_owner(owner, core, spot, hops, h, sibling)
        count = jnp.where(part >= 0, table[count_at + jnp.maximum(part, 0)], 0)

        def take(i, carry, part=part, total=total, n=n):
            entry = table[list_at + part * LIST + i]
            rest = entry // sec_dev
            found[0, total + i] = n
            found[1, total + i] = rest // ops_dev
            found[2, total + i] = lax.rem(rest, ops_dev)
            found[3, total + i] = lax.rem(entry, sec_dev)
            return carry

        lax.fori_loop(0, count, take, 0)
        total = total + count

    def drain(side):
        pltpu.make_async_copy(result.at[side], result.at[side], out_sem.at[side]).wait()

    def grown_of(i):
        which, s, o, local = (found[k, i] for k in range(4))
        block = grounds[0][s]
        for n in range(1, len(parts)):
            block = jnp.where(which == n, grounds[n][s], block)
        product = jnp.dot(block, op_ref[o], preferred_element_type=jnp.float32).astype(BF16)
        return jnp.dot(product, env[local], preferred_element_type=jnp.float32).astype(BF16)

    def send(i):
        side = lax.rem(i, DEPTH)
        target = out_ref.at[found[2, i], found[3, i]]
        pltpu.make_async_copy(result.at[side], target, out_sem.at[side]).start()

    def step(n, carry):
        i, j = 2 * n, 2 * n + 1
        values = grown_of(i), grown_of(jnp.minimum(j, total - 1))

        @pl.when(n >= 2)
        def _():
            drain(lax.rem(i, DEPTH))
            drain(lax.rem(j, DEPTH))

        result[lax.rem(i, DEPTH)] = values[0]
        result[lax.rem(j, DEPTH)] = values[1]
        send(i)
        pl.when(j < total)(lambda: send(j))
        return carry

    steps = (total + 1) // 2
    lax.fori_loop(0, steps, step, 0)
    left = total - 2 * jnp.maximum(steps - 2, 0)
    for back in range(1, DEPTH + 1):
        pl.when(left >= back)(lambda back=back: drain(lax.rem(total - back, DEPTH)))


def finish(dims, table, parts, grounds, op_matrices, env, out, cost):
    ops, sectors, sec_dev, terms = dims
    ops_dev, _, rows, columns = out.shape
    return pl.pallas_call(
        functools.partial(finish_kernel, dims, ops_dev, parts),
        out_shape=jax.ShapeDtypeStruct(out.shape, BF16),
        in_specs=[SMEM] + [VMEM] * (len(parts) + 2) + [ANY],
        out_specs=ANY,
        scratch_shapes=[
            pltpu.SMEM((4, LIST * len(parts)), jnp.int32),
            pltpu.VMEM((DEPTH, rows, columns), BF16),
            pltpu.SemaphoreType.DMA((DEPTH,)),
        ],
        input_output_aliases={len(parts) + 3: 0},
        compiler_params=pltpu.CompilerParams(vmem_limit_bytes=MEDIUM),
        cost_estimate=pl.CostEstimate(flops=cost, bytes_accessed=1 << 12, transcendentals=0),
        name="finish",
    )(table, *grounds, op_matrices, env, out)


def line_of_four(ground_state, op_matrices, shift_map, new_slot, env_ground, env_src, env_coef):
    _, _, spot = device_place()
    sec_dev, rows, columns = ground_state.shape
    ops, sectors = shift_map.shape
    ops_dev = op_matrices.shape[0]
    dims = (ops, sectors, sec_dev, env_src.shape[1])
    half = rows // 2

    def stream(steps):
        up = [(2 * a, 2 * a + 2) for a in steps]
        down = [(2 * (3 - a) + 1, 2 * (2 - a) + 1) for a in steps]
        return lambda block: lax.ppermute(block, ("sec", "op"), up + down)

    def hand(block, spots):
        pairs_of = [(2 * z + core, 2 * z + 1 - core) for spot in spots for z, core in at[spot]]
        return lax.ppermute(block, ("sec", "op"), pairs_of)

    def across(block):
        leads = at[2] + at[3]
        pairs_of = [((z * 2 + x) * 2 + core, (z * 2 + 1 - x) * 2 + 1 - core) for z, core in leads for x in range(2)]
        return lax.ppermute(block, ("sec", "blk", "op"), pairs_of)

    def after(block, *others):
        return lax.optimization_barrier((block, *others))[0]

    at = [[(0, 0), (3, 1)], [(1, 0), (2, 1)], [(2, 0), (1, 1)], [(3, 0), (0, 1)]]
    every, middle, late, last = stream([0, 1, 2]), stream([1]), stream([1, 2]), stream([2])
    ground_half = ground_state.reshape(2, sec_dev, half, columns)
    both = range(2)

    sent0 = [head(h, env_ground, ground_half) for h in both]
    got0 = [every(sent0[h]) for h in both]
    got2 = [middle(got0[h]) for h in both]
    swapped0 = [hand(got0[h], [1, 3]) for h in both]
    table = tables(dims, ops_dev, shift_map, new_slot, env_src.T)
    sent4, made = zip(
        *[blend(dims, h, table, env_coef.T, got2[h], got0[h], env_ground, swapped0[h], ground_half) for h in both]
    )
    got4 = [every(sent4[h]) for h in both]
    near = [hand(made[h], [2]) for h in both]
    got6 = [late(got4[0]), late(after(got4[1], *near))]
    swapped4 = [hand(got4[h], [1, 2, 3]) for h in both]
    swapped6 = [hand(got6[0], [2, 3])]
    far = [across(jnp.where(spot == 2, made[h], got4[h])) for h in both]
    back = [hand(after(far[h], got6[0]), [0, 1]) for h in both]
    got8 = [last(got6[0]), last(after(got6[1], *swapped4, swapped6[0], back[0]))]
    pieces = [block[h] for h in both for block in (made, near, got4, swapped4, far, back)]

    parts = [(0, None, h, False, h * sec_dev // 2) for h in both]
    arrays = [ground_state]

    def blocks(block):
        return block.reshape(sec_dev // 2, rows, columns)

    def hold(mine, theirs, hops, h):
        for block, sibling in ((mine, False), (theirs, True)):
            parts.append((len(arrays), hops, h, sibling, 0))
            arrays.append(blocks(block))

    for h in both:
        hold(got0[h], swapped0[h], [0, 0, 0, 1], h)
        hold(got4[h], swapped4[h], [0, 1, 1, 0], h)
    hold(got6[0], swapped6[0], [0, 0, 2, 2], 0)
    parts.append((len(arrays), [0, 0, 2, 2], 1, False, 0))
    arrays.append(blocks(got6[1]))
    out, env = grow(dims, table, parts, arrays, op_matrices, pieces)
    swapped6.append(hand(after(got6[1], out), [2, 3]))
    swapped8 = [hand(after(got8[h], out), [3]) for h in both]
    ends, owners = [blocks(swapped6[1])], [([0, 0, 2, 2], 1, True)]
    for h in both:
        ends += [blocks(got8[h]), blocks(swapped8[h])]
        owners += [([0, 0, 0, 3], h, False), ([0, 0, 0, 3], h, True)]
        out = finish(dims, table, owners, ends, op_matrices, env, out, 1 << 20)
        ends, owners = [], []
    return out


def solution(mesh):
    four = mesh.shape["sec"] == 4 and mesh.shape["blk"] == 2 and mesh.shape["op"] == 2
    return jax.shard_map(
        line_of_four if four else whole_gather,
        mesh=mesh,
        in_specs=(
            P(("grp", "sec"), "blk", None),
            P(("grp", "op"), None, None),
            P("grp", None),
            P("grp"),
            P(("grp", "sec"), "blk", None),
            P("grp", None),
            P("grp", None),
        ),
        out_specs=P(("grp", "op"), "sec", "blk", None),
        check_vma=False,
    )
```
